32 devices in a mesh: dp: 16 (over z, x, core), mp: 2 (over y).
Axes of the slice: x: 2, y: 2, z: 4, core: 2. Of those that a mesh axis runs over, the one named last changes fastest.
Arguments:
- inputs: bfloat16 [16384, 2048], P('dp'), may hold values from -6 to 6
- prefix_len: int32 [16], P('dp'), may hold values from 102 to 512, as said below
- norm1_gain: float32 [2048], replicated, may hold values from 0.1 to 1.9
- norm1_bias: float32 [2048], replicated, may hold values from -4 to 4
- query_weight: bfloat16 [2048, 2048], P(None, 'mp'), may hold values from -0.25 to 0.25
- query_bias: float32 [16, 128], P('mp'), may hold values from -6 to 6
- key_weight: bfloat16 [2048, 2048], P(None, 'mp'), may hold values from -0.125 to 0.125
- value_weight: bfloat16 [2048, 2048], P(None, 'mp'), may hold values from -0.125 to 0.125
- value_bias: float32 [16, 128], P('mp'), may hold values from -6 to 6
- out_weight: bfloat16 [2048, 2048], P('mp'), may hold values from -0.5 to 0.5
- out_bias: float32 [2048], replicated, may hold values from -4 to 4
- norm2_gain: float32 [2048], replicated, may hold values from 0.1 to 1.9
- norm2_bias: float32 [2048], replicated, may hold values from -4 to 4
- up_weight: bfloat16 [2048, 8192], P(None, 'mp'), may hold values from -0.125 to 0.125
- up_bias: float32 [64, 128], P('mp'), may hold values from -6 to 6
- down_weight: bfloat16 [8192, 2048], P('mp'), may hold values from -0.0625 to 0.0625
- down_bias: float32 [2048], replicated, may hold values from -4 to 4
- out_grad: bfloat16 [16384, 2048], P('dp'), may hold values from -6 to 6
Outputs:
- outputs: bfloat16 [16384, 2048], P('dp')
- in_grad: bfloat16 [16384, 2048], P('dp')
- norm1_gain_grad: float32 [2048], P('dp')
- norm1_bias_grad: float32 [2048], P('dp')
- query_weight_grad: float32 [2048, 2048], P('dp', 'mp')
- query_bias_grad: float32 [16, 128], P('mp', 'dp')
- key_weight_grad: float32 [2048, 2048], P('dp', 'mp')
- value_weight_grad: float32 [2048, 2048], P('dp', 'mp')
- value_bias_grad: float32 [16, 128], P('mp', 'dp')
- out_weight_grad: float32 [2048, 2048], P('mp', 'dp')
- out_bias_grad: float32 [2048], P('dp')
- norm2_gain_grad: float32 [2048], P('dp')
- norm2_bias_grad: float32 [2048], P('dp')
- up_weight_grad: float32 [2048, 8192], P('dp', 'mp')
- up_bias_grad: float32 [64, 128], P('mp', 'dp')
- down_weight_grad: float32 [8192, 2048], P('mp', 'dp')
- down_bias_grad: float32 [2048], P('dp')
The draws below stay inside these ranges and needn't reach their ends.
Inputs may be any that keep to these rules, and one draw needn't show every extreme that they name: `prefix_len`: each sequence's prefix length; some sequence has exactly 512 and some exactly 102 in every draw.
All inputs are finite; a program needn't handle non-finite values.
Results may differ from the reference program's by a relative error of at most 0.014.
The reference program's roundings to bfloat16 on the way count: a program that leaves them out, or rounds other values in their place, can miss the bound.
Values sent between devices are 32-bit elements; how exact they have to be, the bound alone decides.
No kernel may reach another device: no remote copies, remote signals or barrier semaphores. Data moves between devices by JAX's collectives and lax.ppermute only.
A program may use at most 384 MiB of HBM per device.

```python
import math
import jax
import jax.numpy as jnp
from jax import lax

D = 2048
HEADS = 16
HEAD_DIM = 128
FF = 8192
SEQ_LEN = 1024
SEQS = 16
TOKENS = 16384


def draw_prefix_len(key, part):
    lowest = SEQ_LEN // 10
    highest = SEQ_LEN // 2
    first, second, third = jax.random.split(key, 3)
    lengths = jax.random.randint(first, (SEQS,), lowest, highest + 1)
    top_at = jax.random.randint(second, (), 0, SEQS)
    low_at = (top_at + 1 + jax.random.randint(third, (), 0, SEQS - 1)) % SEQS
    return lengths.at[top_at].set(highest).at[low_at].set(lowest).astype(jnp.int32)


def steps_of(own_key, shape, pieces, least, top_value):
    loudness = 1.0
    for dim, parts in pieces:
        heights = jax.random.uniform(jax.random.fold_in(jax.random.fold_in(own_key, 6), dim), (parts,), jnp.float32, least / len(pieces), top_value / len(pieces))
        loudness = loudness * jnp.repeat(jnp.exp(heights), shape[dim] // parts).reshape((-1,) + (1,) * (len(shape) - 1 - dim))
    return loudness


def bell_draw(stream_key, shape, deviation, limit, pieces=(), held_as=jnp.bfloat16):
    values = jax.random.normal(stream_key, shape, jnp.float32) * deviation
    if len(pieces) > 0:
        values = steps_of(stream_key, shape, pieces, -0.22, 0.18) * values
    return jnp.clip(values, min=-limit, max=limit).astype(held_as)


def setup_inputs(seed: int = 0) -> dict:
    splits = jax.random.split(jax.random.key(seed), 19)
    inputs = bell_draw(splits[0], (TOKENS, D), 1.0, 6.0, ((0, 16),))
    prefix_len = draw_prefix_len(jax.random.fold_in(splits[18], 71), 0)
    norm1_gain = jnp.clip(1.0 + 0.18 * jax.random.normal(splits[2], (D,), jnp.float32), 0.1, 1.9)
    norm1_bias = bell_draw(splits[3], (D,), 0.3, 4.0, (), jnp.float32)
    query_weight = bell_draw(splits[4], (D, HEADS * HEAD_DIM), (D // 4) ** -0.5, 0.25, ((1, 2),))
    query_bias = bell_draw(splits[5], (HEADS, HEAD_DIM), 0.5, 6.0, ((0, 2),), jnp.float32)
    key_weight = bell_draw(splits[6], (D, HEADS * HEAD_DIM), D ** -0.5, 0.125, ((1, 2),))
    value_weight = bell_draw(splits[7], (D, HEADS * HEAD_DIM), D ** -0.5, 0.125, ((1, 2),))
    value_bias = bell_draw(splits[8], (HEADS, HEAD_DIM), 0.5, 6.0, ((0, 2),), jnp.float32)
    out_weight = bell_draw(splits[9], (HEADS * HEAD_DIM, D), (HEADS * HEAD_DIM // 16) ** -0.5, 0.5, ((0, 2),))
    out_bias = bell_draw(splits[10], (D,), 0.3, 4.0, (), jnp.float32)
    norm2_gain = jnp.clip(1.0 + 0.18 * jax.random.normal(splits[11], (D,), jnp.float32), 0.1, 1.9)
    norm2_bias = bell_draw(splits[12], (D,), 0.3, 4.0, (), jnp.float32)
    up_weight = bell_draw(splits[13], (D, FF), D ** -0.5, 0.125, ((1, 2),))
    up_bias = bell_draw(splits[14], (FF // 128, 128), 0.5, 6.0, ((0, 2),), jnp.float32)
    down_weight = bell_draw(splits[15], (FF, D), FF ** -0.5, 0.0625, ((0, 2),))
    down_bias = bell_draw(splits[16], (D,), 0.3, 4.0, (), jnp.float32)
    out_grad = bell_draw(splits[17], (TOKENS, D), 1.0, 6.0, ((0, 16),))
    return {"inputs": inputs, "prefix_len": prefix_len, "norm1_gain": norm1_gain, "norm1_bias": norm1_bias, "query_weight": query_weight, "query_bias": query_bias, "key_weight": key_weight, "value_weight": value_weight, "value_bias": value_bias, "out_weight": out_weight, "out_bias": out_bias, "norm2_gain": norm2_gain, "norm2_bias": norm2_bias, "up_weight": up_weight, "up_bias": up_bias, "down_weight": down_weight, "down_bias": down_bias, "out_grad": out_grad}


HIGH = lax.Precision.HIGHEST

@jax.custom_vjp
def low(v):
    return lax.optimization_barrier(v.astype(jnp.bfloat16)).astype(jnp.float32)

@jax.custom_vjp
def low_back(v):
    return v

def low_keep(v):
    return (low(v), None)

def low_pass(kept, grad):
    return (grad,)

def back_keep(v):
    return (v, None)

def back_low(kept, grad):
    return (low(grad),)
low.defvjp(low_keep, low_pass)
low_back.defvjp(back_keep, back_low)

def layer_norm(field, norm_gain, norm_bias):
    average = lax.optimization_barrier(jnp.mean(field, -1, keepdims=True))
    centred = field - average
    variance = lax.optimization_barrier(jnp.mean(centred * centred, -1, keepdims=True))
    return centred * lax.rsqrt(variance + 1e-05) * norm_gain + norm_bias

def project(field, matrix):
    return jnp.einsum('gld,de->gle', field, matrix, precision=HIGH)

def forward(params, features, lengths):
    norm1_gain, norm1_bias, query_weight, query_bias, key_weight, value_weight, value_bias, out_weight, out_bias, norm2_gain, norm2_bias, up_weight, up_bias, down_weight, down_bias = params
    groups, length, width = features.shape
    heads, head_dim = query_bias.shape
    normed = low(layer_norm(features, norm1_gain, norm1_bias))
    queries = low_back(low(project(normed, query_weight) + query_bias.reshape(-1)))
    keys = low_back(low(project(normed, key_weight)))
    values = low_back(low(project(normed, value_weight) + value_bias.reshape(-1)))
    queries = queries.reshape(groups, length, heads, head_dim)
    keys = keys.reshape(groups, length, heads, head_dim)
    values = values.reshape(groups, length, heads, head_dim)
    block_rows = min(512, length)
    block_count = length // block_rows
    score_scale = 1.0 / math.sqrt(head_dim)
    positions = jnp.arange(length, dtype=jnp.int32)

    def attend(block_index):
        row_begin = block_index * block_rows
        query_block = lax.dynamic_slice_in_dim(queries, row_begin, block_rows, 1)
        raw_scores = jnp.einsum('gqhd,gkhd->ghqk', query_block, keys, precision=HIGH)
        scores = low_back(raw_scores) * score_scale
        rows = row_begin + jnp.arange(block_rows, dtype=jnp.int32)
        visible = (positions[None, None, :] <= rows[None, :, None]) | (positions[None, None, :] < lengths[:, None, None])
        scores = jnp.where(visible[:, None], scores, -1e+30)
        peak = lax.optimization_barrier(jnp.max(scores, -1, keepdims=True))
        exps = jnp.exp(scores - peak)
        probs = low(exps / lax.optimization_barrier(jnp.sum(exps, -1, keepdims=True)))
        return jnp.einsum('ghqk,gkhd->gqhd', probs, values, precision=HIGH)
    mixed = lax.map(jax.checkpoint(attend), jnp.arange(block_count, dtype=jnp.int32))
    mixed = jnp.moveaxis(mixed, 0, 1).reshape(groups, length, heads * head_dim)
    mixed = low_back(low(mixed))
    attn = low_back(project(mixed, out_weight) + out_bias)
    resid = features + attn
    normed2 = low(layer_norm(resid, norm2_gain, norm2_bias))
    hidden = low_back(project(normed2, up_weight) + up_bias.reshape(-1))
    acts = low(jax.nn.gelu(hidden, approximate=False))
    branch = low_back(project(acts, down_weight) + down_bias)
    return resid + branch

def reference(inputs, prefix_len, norm1_gain, norm1_bias, query_weight, query_bias, key_weight, value_weight, value_bias, out_weight, out_bias, norm2_gain, norm2_bias, up_weight, up_bias, down_weight, down_bias, out_grad):
    params = tuple((item.astype(jnp.float32) for item in (norm1_gain, norm1_bias, query_weight, query_bias, key_weight, value_weight, value_bias, out_weight, out_bias, norm2_gain, norm2_bias, up_weight, up_bias, down_weight, down_bias)))
    group_size = math.gcd(SEQS, max(1, 4096 // SEQ_LEN))
    group_count = SEQS // group_size
    features = inputs.astype(jnp.float32).reshape(group_count, group_size, SEQ_LEN, D)
    cotangent = out_grad.astype(jnp.float32).reshape(group_count, group_size, SEQ_LEN, D)
    lengths = prefix_len.reshape(group_count, group_size)

    def step(carry, item):
        piece_in, piece_cot, piece_len = item
        result, pullback = jax.vjp(lambda weights, field: forward(weights, field, piece_len), params, piece_in)
        grads, field_grad = pullback(piece_cot)
        carry = jax.tree.map(lambda left, right: left + right, carry, grads)
        return (carry, (result, field_grad))
    zeros_tree = jax.tree.map(jnp.zeros_like, params)
    totals, (results, field_grads) = lax.scan(step, zeros_tree, (features, cotangent, lengths))
    return (results.reshape(TOKENS, D).astype(jnp.bfloat16), field_grads.reshape(TOKENS, D).astype(jnp.bfloat16), totals[0], totals[1], totals[2], totals[3], totals[4], totals[5], totals[6], totals[7], totals[8], totals[9], totals[10], totals[11], totals[12], totals[13], totals[14])
```

```python
import math

import jax
import jax.numpy as jnp
from jax import lax
from jax.sharding import Mesh
from jax.sharding import PartitionSpec as P

F32 = jnp.float32
BF16 = jnp.bfloat16
CHUNKS = 4


def swap(value, axis):
    return lax.ppermute(value, axis, [(0, 1), (1, 0)])


def mm(left, right, contract):
    return lax.dot_general(left, right, (contract, ((), ())), preferred_element_type=F32)


def norm_parts(field):
    average = jnp.mean(field, -1, keepdims=True)
    centred = field - average
    variance = jnp.mean(centred * centred, -1, keepdims=True)
    scale = lax.rsqrt(variance + 1e-05)
    return centred * scale, scale


def norm_pull(grad, unit, scale, gain):
    scaled = grad * gain
    first = jnp.mean(scaled, -1, keepdims=True)
    second = jnp.mean(scaled * unit, -1, keepdims=True)
    return scale * (scaled - first - unit * second)


def exact_gelu(field):
    return jax.nn.gelu(field, approximate=False)


def body(
    inputs,
    prefix_len,
    norm1_gain,
    norm1_bias,
    query_weight,
    query_bias,
    key_weight,
    value_weight,
    value_bias,
    out_weight,
    out_bias,
    norm2_gain,
    norm2_bias,
    up_weight,
    up_bias,
    down_weight,
    down_bias,
    out_grad,
):
    length, width = inputs.shape
    heads_local, head_dim = query_bias.shape
    zs, xs, cs = lax.axis_size("z"), lax.axis_size("x"), lax.axis_size("c")
    dps = zs * xs * cs
    at_x, at_c = lax.axis_index("x"), lax.axis_index("c")
    here, over_x = at_x * 2 + at_c, (1 - at_x) * 2 + at_c
    over_c, over_xc = at_x * 2 + 1 - at_c, (1 - at_x) * 2 + 1 - at_c
    block_rows = min(512, length)
    block_count = length // block_rows
    chunk = length // CHUNKS
    score_scale = 1.0 / math.sqrt(head_dim)
    boundary = prefix_len[0]

    def pieces(field):
        parts = field.reshape(length, zs, xs * cs, width // dps)
        return jnp.transpose(parts, (2, 0, 1, 3)).reshape(xs * cs, length, width // (xs * cs))

    def reduce_weight(parts, other, by_rows):
        def part(index):
            piece = lax.dynamic_index_in_dim(parts, index, 0, keepdims=False)
            if by_rows:
                return mm(piece, other, ((0,), (0,)))
            return mm(other, piece, ((0,), (0,)))

        far = swap(part(over_xc), "c")
        near = swap(part(over_c), "c")
        across = swap(part(over_x) + far, "x")
        total = part(here) + near + across
        return lax.psum_scatter(total, "z", scatter_dimension=0 if by_rows else 1, tiled=True)

    features = inputs.astype(F32)
    unit1, scale1 = norm_parts(features)
    normed = (unit1 * norm1_gain + norm1_bias).astype(BF16)
    queries = (mm(normed, query_weight, ((1,), (0,))) + query_bias.reshape(-1)).astype(BF16)
    keys = mm(normed, key_weight, ((1,), (0,))).astype(BF16)
    values = (mm(normed, value_weight, ((1,), (0,))) + value_bias.reshape(-1)).astype(BF16)
    queries = queries.reshape(length, heads_local, head_dim)
    keys = keys.reshape(length, heads_local, head_dim)
    values = values.reshape(length, heads_local, head_dim)

    def block_scores(row_begin, seen):
        query_block = queries[row_begin : row_begin + block_rows]
        scores = (
            jnp.einsum("qhd,khd->hqk", query_block, keys[:seen], preferred_element_type=F32)
            * score_scale
        )
        rows = row_begin + jnp.arange(block_rows, dtype=jnp.int32)
        positions = jnp.arange(seen, dtype=jnp.int32)
        visible = (positions[None, :] <= rows[:, None]) | (positions[None, :] < boundary)
        return (query_block, jnp.where(visible[None], scores, -1e30))

    mixed_blocks = []
    totals_log = []
    attn_parts = []
    for block_index in range(block_count):
        row_begin = block_index * block_rows
        seen = max(row_begin + block_rows, length // 2)
        query_block, scores = block_scores(row_begin, seen)
        peak = jnp.max(scores, -1, keepdims=True)
        exps = jnp.exp(scores - peak)
        sums = jnp.sum(exps, -1, keepdims=True)
        probs = exps / sums
        totals_log.append(peak + jnp.log(sums))
        mixed_block = (
            jnp.einsum(
                "hqk,khd->qhd", probs.astype(BF16), values[:seen], preferred_element_type=F32
            )
            .astype(BF16)
            .reshape(block_rows, heads_local * head_dim)
        )
        mixed_blocks.append(mixed_block)
        for begin in range(0, block_rows, chunk):
            attn_parts.append(mm(mixed_block[begin : begin + chunk], out_weight, ((1,), (0,))))
    mixed = jnp.concatenate(mixed_blocks, 0)
    attn_others = [swap(part, "mp") for part in attn_parts]

    resids, units2, scales2, normeds2, acts, hidden_grads = [], [], [], [], [], []
    norm2_parts, branch_parts, up_bias_grad = [], [], 0.0
    for index in range(CHUNKS):
        rows = slice(index * chunk, (index + 1) * chunk)
        resid = features[rows] + ((attn_parts[index] + attn_others[index]) + out_bias)
        unit2, scale2 = norm_parts(resid)
        normed2 = (unit2 * norm2_gain + norm2_bias).astype(BF16)
        hidden = mm(normed2, up_weight, ((1,), (0,))) + up_bias.reshape(-1)
        acts_float, gelu_pull = jax.vjp(exact_gelu, hidden)
        act = acts_float.astype(BF16)
        acts_grad = mm(out_grad[rows], down_weight, ((1,), (1,)))
        hidden_grad = gelu_pull(acts_grad)[0].astype(BF16)
        up_bias_grad = up_bias_grad + jnp.sum(hidden_grad.astype(F32), 0)
        norm2_parts.append(mm(hidden_grad, up_weight, ((1,), (1,))))
        branch_parts.append(mm(act, down_weight, ((1,), (0,))))
        resids.append(resid)
        units2.append(unit2)
        scales2.append(scale2)
        normeds2.append(normed2)
        acts.append(act)
        hidden_grads.append(hidden_grad)
    norm2_others = [swap(part, "mp") for part in norm2_parts]
    branch_others = [swap(part, "mp") for part in branch_parts]

    acts = jnp.concatenate(acts, 0)
    hidden_grads = jnp.concatenate(hidden_grads, 0)
    normed2 = jnp.concatenate(normeds2, 0)
    down_weight_grad = reduce_weight(pieces(out_grad), acts, False)
    up_weight_grad = reduce_weight(pieces(normed2), hidden_grads, True)

    grad_float = out_grad.astype(F32)
    down_bias_grad = jnp.sum(grad_float, 0)

    resid_grads, attn_grads, mixed_grads = [], [], []
    norm2_gain_grad, norm2_bias_grad, out_bias_grad = 0.0, 0.0, 0.0
    for index in range(CHUNKS):
        rows = slice(index * chunk, (index + 1) * chunk)
        norm2_in = norm2_parts[index] + norm2_others[index]
        norm2_bias_grad = norm2_bias_grad + jnp.sum(norm2_in, 0)
        norm2_gain_grad = norm2_gain_grad + jnp.sum(norm2_in * units2[index], 0)
        resid_grad = grad_float[rows] + norm_pull(norm2_in, units2[index], scales2[index], norm2_gain)
        attn_grad = resid_grad.astype(BF16)
        out_bias_grad = out_bias_grad + jnp.sum(attn_grad.astype(F32), 0)
        mixed_grads.append(mm(attn_grad, out_weight, ((1,), (1,))).astype(BF16))
        resid_grads.append(resid_grad)
        attn_grads.append(attn_grad)
    mixed_grad = jnp.concatenate(mixed_grads, 0).reshape(length, heads_local, head_dim)
    attn_grad = jnp.concatenate(attn_grads, 0)
    out_weight_grad = reduce_weight(pieces(attn_grad), mixed, False)

    query_blocks = []
    key_accum = jnp.zeros((length, heads_local, head_dim), F32)
    value_accum = jnp.zeros((length, heads_local, head_dim), F32)
    for block_index in range(block_count):
        row_begin = block_index * block_rows
        seen = max(row_begin + block_rows, length // 2)
        query_block, scores = block_scores(row_begin, seen)
        probs = jnp.exp(scores - totals_log[block_index])
        mixed_block = mixed_grad[row_begin : row_begin + block_rows]
        prob_grad = jnp.einsum(
            "qhd,khd->hqk", mixed_block, values[:seen], preferred_element_type=F32
        )
        row_dot = jnp.sum(probs * prob_grad, -1, keepdims=True)
        score_grad = (probs * (prob_grad - row_dot) * score_scale).astype(BF16)
        query_blocks.append(
            jnp.einsum("hqk,khd->qhd", score_grad, keys[:seen], preferred_element_type=F32)
        )
        key_accum = key_accum.at[:seen].add(
            jnp.einsum("hqk,qhd->khd", score_grad, query_block, preferred_element_type=F32)
        )
        value_accum = value_accum.at[:seen].add(
            jnp.einsum("hqk,qhd->khd", probs.astype(BF16), mixed_block, preferred_element_type=F32)
        )
    flat = (length, heads_local * head_dim)
    query_grad = jnp.concatenate(query_blocks, 0).astype(BF16).reshape(flat)
    key_grad = key_accum.astype(BF16).reshape(flat)
    value_grad = value_accum.astype(BF16).reshape(flat)
    query_bias_grad = jnp.sum(query_grad.astype(F32), 0)
    value_bias_grad = jnp.sum(value_grad.astype(F32), 0)

    norm1_parts = []
    norm1_gain_grad, norm1_bias_grad = 0.0, 0.0
    for index in range(CHUNKS):
        rows = slice(index * chunk, (index + 1) * chunk)
        part = mm(query_grad[rows], query_weight, ((1,), (1,)))
        part = part + mm(key_grad[rows], key_weight, ((1,), (1,)))
        part = part + mm(value_grad[rows], value_weight, ((1,), (1,)))
        norm1_parts.append(part)
        norm1_bias_grad = norm1_bias_grad + jnp.sum(part, 0)
        norm1_gain_grad = norm1_gain_grad + jnp.sum(part * unit1[rows], 0)
    norm1_others = [swap(part, "mp") for part in norm1_parts]

    normed_pieces = pieces(normed)
    query_weight_grad = reduce_weight(normed_pieces, query_grad, True)
    key_weight_grad = reduce_weight(normed_pieces, key_grad, True)
    value_weight_grad = reduce_weight(normed_pieces, value_grad, True)

    def blocks(vector, lead):
        return jnp.transpose(vector.reshape(lead, dps, -1), (1, 0, 2)).reshape(dps, -1)

    shared = jnp.concatenate([blocks(norm1_gain_grad, 1), blocks(norm1_bias_grad, 1)], 1)
    shared = shared + swap(shared, "mp")
    small = jnp.concatenate(
        [
            shared,
            blocks(query_bias_grad, heads_local),
            blocks(value_bias_grad, heads_local),
            blocks(out_bias_grad, 1),
            blocks(norm2_gain_grad, 1),
            blocks(norm2_bias_grad, 1),
            blocks(up_bias_grad, up_bias.shape[0]),
            blocks(down_bias_grad, 1),
        ],
        1,
    )
    small = small.reshape(zs, xs * cs, -1)

    def take(field, index, axis):
        return lax.dynamic_index_in_dim(field, index, axis, keepdims=False)

    far = swap(jnp.stack([take(small, over_xc, 1), take(small, over_c, 1)]), "c")
    across = swap(take(small, over_x, 1) + far[0], "x")
    small = take(small, here, 1) + far[1] + across
    at_z, span = lax.axis_index("z"), zs
    while span > 1:
        span //= 2
        halves = small.reshape(2, span, -1)
        side = (at_z // span) % 2
        pairs = [(i, i ^ span) for i in range(zs)]
        other = lax.ppermute(take(halves, 1 - side, 0), "z", pairs)
        small = take(halves, side, 0) + other
    small = small.reshape(-1)

    in_grads, outputs = [], []
    for index in range(CHUNKS):
        rows = slice(index * chunk, (index + 1) * chunk)
        outputs.append(
            (resids[index] + ((branch_parts[index] + branch_others[index]) + down_bias)).astype(BF16)
        )
        norm1_in = norm1_parts[index] + norm1_others[index]
        pulled = norm_pull(norm1_in, unit1[rows], scale1[rows], norm1_gain)
        in_grads.append((resid_grads[index] + pulled).astype(BF16))
    outputs = jnp.concatenate(outputs, 0)
    in_grad = jnp.concatenate(in_grads, 0)

    wide = width // dps
    thin = head_dim // dps
    sizes = [wide, wide, heads_local * thin, heads_local * thin, wide, wide, wide]
    sizes += [up_bias.shape[0] * thin, wide]
    split, begin = [], 0
    for size in sizes:
        split.append(small[begin : begin + size])
        begin += size
    gain1, bias1, query_b, value_b, out_b, gain2, bias2, up_b, down_b = split
    return (
        outputs,
        in_grad,
        gain1,
        bias1,
        query_weight_grad,
        query_b.reshape(heads_local, thin),
        key_weight_grad,
        value_weight_grad,
        value_b.reshape(heads_local, thin),
        out_weight_grad,
        out_b,
        gain2,
        bias2,
        up_weight_grad,
        up_b.reshape(-1, thin),
        down_weight_grad,
        down_b,
    )


def solution(mesh):
    dps = mesh.shape["dp"]
    fine = Mesh(mesh.devices.reshape(dps // 4, 2, 2, mesh.shape["mp"]), ("z", "x", "c", "mp"))
    dp = ("z", "x", "c")
    in_specs = (
        P(dp, None),
        P(dp),
        P(),
        P(),
        P(None, "mp"),
        P("mp", None),
        P(None, "mp"),
        P(None, "mp"),
        P("mp", None),
        P("mp", None),
        P(),
        P(),
        P(),
        P(None, "mp"),
        P("mp", None),
        P("mp", None),
        P(),
        P(dp, None),
    )
    out_specs = (
        P(dp, None),
        P(dp, None),
        P(dp),
        P(dp),
        P(dp, "mp"),
        P("mp", dp),
        P(dp, "mp"),
        P(dp, "mp"),
        P("mp", dp),
        P("mp", dp),
        P(dp),
        P(dp),
        P(dp),
        P(dp, "mp"),
        P("mp", dp),
        P("mp", dp),
        P(dp),
    )
    return jax.shard_map(body, mesh=fine, in_specs=in_specs, out_specs=out_specs, check_vma=False)
```

```python
import math

import jax
import jax.numpy as jnp
from jax import lax
from jax.sharding import Mesh
from jax.sharding import PartitionSpec as P

F32 = jnp.float32
BF16 = jnp.bfloat16
CHUNKS = 4


def swap(value, axis):
    return lax.ppermute(value, axis, [(0, 1), (1, 0)])


def mm(left, right, contract):
    return lax.dot_general(left, right, (contract, ((), ())), preferred_element_type=F32)


def norm_parts(field):
    average = jnp.mean(field, -1, keepdims=True)
    centred = field - average
    variance = jnp.mean(centred * centred, -1, keepdims=True)
    scale = lax.rsqrt(variance + 1e-05)
    return centred * scale, scale


def norm_pull(grad, unit, scale, gain):
    scaled = grad * gain
    first = jnp.mean(scaled, -1, keepdims=True)
    second = jnp.mean(scaled * unit, -1, keepdims=True)
    return scale * (scaled - first - unit * second)


def after(value, *others):
    return lax.optimization_barrier((value,) + others)[0]


def exact_gelu(field):
    return jax.nn.gelu(field, approximate=False)


def body(
    inputs,
    prefix_len,
    norm1_gain,
    norm1_bias,
    query_weight,
    query_bias,
    key_weight,
    value_weight,
    value_bias,
    out_weight,
    out_bias,
    norm2_gain,
    norm2_bias,
    up_weight,
    up_bias,
    down_weight,
    down_bias,
    out_grad,
):
    length, width = inputs.shape
    heads_local, head_dim = query_bias.shape
    zs, xs, cs = lax.axis_size("z"), lax.axis_size("x"), lax.axis_size("c")
    dps = zs * xs * cs
    at_x, at_c = lax.axis_index("x"), lax.axis_index("c")
    wide = width // dps
    part = zs * wide
    block_rows = min(512, length)
    block_count = length // block_rows
    chunk = length // CHUNKS
    score_scale = 1.0 / math.sqrt(head_dim)
    boundary = prefix_len[0]

    def pieces(field):
        order = [(z * xs + x) * cs + c for c in range(cs) for x in range(xs) for z in range(zs)]
        return jnp.concatenate([field[:, at * wide : (at + 1) * wide] for at in order], 1)

    class Sum:
        def __init__(self, parts, other, by_rows):
            self.parts, self.other, self.by_rows = parts, other, by_rows
            self.dim = 0 if by_rows else 1

        def product(self, begin, size, gate):
            piece = lax.dynamic_slice_in_dim(self.parts, begin, size, 1)
            other = after(self.other, *gate)
            if self.by_rows:
                return mm(piece, other, ((0,), (0,)))
            return mm(other, piece, ((0,), (0,)))

        def arrived(self, x):
            return lax.dynamic_slice_in_dim(self.near, x * part, part, self.dim)

        def over_cores(self, *gate):
            own = self.product((1 - at_c) * xs * part, xs * part, gate)
            self.near = swap(own, "c")
            return own

        def over_x(self, *gate):
            far = 1 - at_x
            own = self.product((at_c * xs + far) * part, part, gate) + self.arrived(far)
            self.across = swap(own, "x")
            return own

        def over_z(self, *gate):
            own = self.product((at_c * xs + at_x) * part, part, gate) + self.arrived(at_x)
            total = own + self.across
            self.result = lax.psum_scatter(total, "z", scatter_dimension=self.dim, tiled=True)
            return total

    features = inputs.astype(F32)
    unit1, scale1 = norm_parts(features)
    normed = (unit1 * norm1_gain + norm1_bias).astype(BF16)
    queries = (mm(normed, query_weight, ((1,), (0,))) + query_bias.reshape(-1)).astype(BF16)
    keys = mm(normed, key_weight, ((1,), (0,))).astype(BF16)
    values = (mm(normed, value_weight, ((1,), (0,))) + value_bias.reshape(-1)).astype(BF16)
    queries = queries.reshape(length, heads_local, head_dim)
    keys = keys.reshape(length, heads_local, head_dim)
    values = values.reshape(length, heads_local, head_dim)

    def block_scores(row_begin, seen):
        query_block = queries[row_begin : row_begin + block_rows]
        scores = (
            jnp.einsum("qhd,khd->hqk", query_block, keys[:seen], preferred_element_type=F32)
            * score_scale
        )
        rows = row_begin + jnp.arange(block_rows, dtype=jnp.int32)
        positions = jnp.arange(seen, dtype=jnp.int32)
        visible = (positions[None, :] <= rows[:, None]) | (positions[None, :] < boundary)
        return (query_block, jnp.where(visible[None], scores, -1e30))

    mixed_blocks = []
    totals_log = []
    attn_parts = []
    for block_index in range(block_count):
        row_begin = block_index * block_rows
        seen = max(row_begin + block_rows, length // 2)
        query_block, scores = block_scores(row_begin, seen)
        peak = jnp.max(scores, -1, keepdims=True)
        exps = jnp.exp(scores - peak)
        sums = jnp.sum(exps, -1, keepdims=True)
        probs = exps / sums
        totals_log.append(peak + jnp.log(sums))
        mixed_block = (
            jnp.einsum(
                "hqk,khd->qhd", probs.astype(BF16), values[:seen], preferred_element_type=F32
            )
            .astype(BF16)
            .reshape(block_rows, heads_local * head_dim)
        )
        mixed_blocks.append(mixed_block)
        for begin in range(0, block_rows, chunk):
            attn_parts.append(mm(mixed_block[begin : begin + chunk], out_weight, ((1,), (0,))))
    mixed = jnp.concatenate(mixed_blocks, 0)
    attn_others = [swap(part, "mp") for part in attn_parts]

    resids, units2, scales2, normeds2, acts, hidden_grads = [], [], [], [], [], []
    norm2_parts, up_bias_grad = [], 0.0
    for index in range(CHUNKS):
        rows = slice(index * chunk, (index + 1) * chunk)
        attn_other = attn_others[index]
        if index > 0:
            attn_other = after(attn_other, norm2_parts[index - 1], hidden_grads[index - 1])
        resid = features[rows] + ((attn_parts[index] + attn_other) + out_bias)
        unit2, scale2 = norm_parts(resid)
        normed2 = (unit2 * norm2_gain + norm2_bias).astype(BF16)
        hidden = mm(normed2, up_weight, ((1,), (0,))) + up_bias.reshape(-1)
        acts_float, gelu_pull = jax.vjp(exact_gelu, hidden)
        act = acts_float.astype(BF16)
        acts_grad = mm(out_grad[rows], down_weight, ((1,), (1,)))
        hidden_grad = gelu_pull(acts_grad)[0].astype(BF16)
        up_bias_grad = up_bias_grad + jnp.sum(hidden_grad.astype(F32), 0)
        norm2_parts.append(mm(hidden_grad, up_weight, ((1,), (1,))))
        resids.append(resid)
        units2.append(unit2)
        scales2.append(scale2)
        normeds2.append(normed2)
        acts.append(act)
        hidden_grads.append(hidden_grad)
    norm2_others = [swap(piece, "mp") for piece in norm2_parts]

    grad_float = out_grad.astype(F32)
    down_bias_grad = jnp.sum(grad_float, 0)
    half = up_weight.shape[1] // 2
    halves = [slice(0, half), slice(half, 2 * half)]
    grad_pieces = pieces(out_grad)
    normed2_pieces = pieces(jnp.concatenate(normeds2, 0))
    downs = [Sum(grad_pieces, jnp.concatenate([act[:, cut] for act in acts], 0), False) for cut in halves]
    ups = [
        Sum(normed2_pieces, jnp.concatenate([pull[:, cut] for pull in hidden_grads], 0), True)
        for cut in halves
    ]

    resid_grads, attn_grads, mixed_grads = [], [], []
    norm2_gain_grad, norm2_bias_grad, out_bias_grad = 0.0, 0.0, 0.0

    def norm2_pull(index, *gate):
        nonlocal norm2_gain_grad, norm2_bias_grad, out_bias_grad
        rows = slice(index * chunk, (index + 1) * chunk)
        norm2_in = norm2_parts[index] + after(norm2_others[index], *gate)
        norm2_bias_grad = norm2_bias_grad + jnp.sum(norm2_in, 0)
        norm2_gain_grad = norm2_gain_grad + jnp.sum(norm2_in * units2[index], 0)
        resid_grad = grad_float[rows] + norm_pull(norm2_in, units2[index], scales2[index], norm2_gain)
        attn_grad = resid_grad.astype(BF16)
        out_bias_grad = out_bias_grad + jnp.sum(attn_grad.astype(F32), 0)
        mixed_grads.append(mm(attn_grad, out_weight, ((1,), (1,))).astype(BF16))
        resid_grads.append(resid_grad)
        attn_grads.append(attn_grad)
        return mixed_grads[-1]

    def branch_part(index, *gate):
        return mm(after(acts[index], *gate), down_weight, ((1,), (0,)))

    gate = downs[0].over_cores(norm2_parts[-1], hidden_grads[-1], norm2_others[0])
    gate = norm2_pull(0, gate)
    gate = downs[0].over_x(gate)
    gate = downs[1].over_cores(gate, downs[0].near)
    gate = norm2_pull(1, gate)
    gate = downs[1].over_x(gate)
    gate = ups[0].over_cores(gate, downs[1].near)
    branch_parts = [branch_part(0, gate)]
    gate = norm2_pull(2, branch_parts[0], ups[0].near)
    branch_parts += [branch_part(index, gate) for index in range(1, CHUNKS)]
    gate = norm2_pull(3, *branch_parts)
    gate = downs[0].over_z(gate)
    branch = jnp.concatenate(branch_parts, 0)
    branch_other = swap(after(branch, norm2_others[-1]), "mp")
    gate = ups[0].over_x(gate)
    mixed_grad = jnp.concatenate(mixed_grads, 0).reshape(length, heads_local, head_dim)
    attn_grad = jnp.concatenate(attn_grads, 0)

    query_blocks = []
    key_accum = jnp.zeros((length, heads_local, head_dim), F32)
    value_accum = jnp.zeros((length, heads_local, head_dim), F32)
    for block_index in range(block_count):
        row_begin = block_index * block_rows
        seen = max(row_begin + block_rows, length // 2)
        query_block, scores = block_scores(row_begin, seen)
        probs = jnp.exp(scores - totals_log[block_index])
        mixed_block = after(mixed_grad[row_begin : row_begin + block_rows], gate)
        prob_grad = jnp.einsum(
            "qhd,khd->hqk", mixed_block, values[:seen], preferred_element_type=F32
        )
        row_dot = jnp.sum(probs * prob_grad, -1, keepdims=True)
        score_grad = (probs * (prob_grad - row_dot) * score_scale).astype(BF16)
        query_blocks.append(
            jnp.einsum("hqk,khd->qhd", score_grad, keys[:seen], preferred_element_type=F32)
        )
        key_accum = key_accum.at[:seen].add(
            jnp.einsum("hqk,qhd->khd", score_grad, query_block, preferred_element_type=F32)
        )
        value_accum = value_accum.at[:seen].add(
            jnp.einsum("hqk,qhd->khd", probs.astype(BF16), mixed_block, preferred_element_type=F32)
        )
        if block_index == 0:
            gate = ups[1].over_cores(query_blocks[0], key_accum, value_accum)
            gate = downs[1].over_z(gate, ups[1].near)
            gate = ups[1].over_x(gate)
    flat = (length, heads_local * head_dim)
    query_grad = jnp.concatenate(query_blocks, 0).astype(BF16).reshape(flat)
    key_grad = key_accum.astype(BF16).reshape(flat)
    value_grad = value_accum.astype(BF16).reshape(flat)
    query_bias_grad = jnp.sum(query_grad.astype(F32), 0)
    value_bias_grad = jnp.sum(value_grad.astype(F32), 0)

    half_rows = length // 2
    norm1_parts = []
    for begin in range(0, length, half_rows):
        rows = slice(begin, begin + half_rows)
        piece = mm(query_grad[rows], query_weight, ((1,), (1,)))
        piece = piece + mm(key_grad[rows], key_weight, ((1,), (1,)))
        piece = piece + mm(value_grad[rows], value_weight, ((1,), (1,)))
        norm1_parts.append(piece)
    norm1_others = [swap(piece, "mp") for piece in norm1_parts]

    normed_pieces = pieces(normed)
    out_sum = Sum(pieces(attn_grad), mixed, False)
    query_sum, key_sum, value_sum = [
        Sum(normed_pieces, pull, True) for pull in (query_grad, key_grad, value_grad)
    ]
    gate = out_sum.over_cores(*norm1_parts)
    gate = ups[0].over_z(gate, branch_other)
    gate = out_sum.over_x(gate)
    outputs = (jnp.concatenate(resids, 0) + ((branch + after(branch_other, gate)) + down_bias)).astype(BF16)
    gate = query_sum.over_cores(outputs)
    gate = ups[1].over_z(gate, query_sum.near)
    gate = query_sum.over_x(gate)
    gate = key_sum.over_cores(gate)

    norm1_gain_grad, norm1_bias_grad = 0.0, 0.0
    in_grads = []

    def norm1_pull(index, gate):
        nonlocal norm1_gain_grad, norm1_bias_grad
        rows = slice(index * half_rows, (index + 1) * half_rows)
        norm1_in = norm1_parts[index] + after(norm1_others[index], gate)
        norm1_bias_grad = norm1_bias_grad + jnp.sum(norm1_in, 0)
        norm1_gain_grad = norm1_gain_grad + jnp.sum(norm1_in * unit1[rows], 0)
        pulled = norm_pull(norm1_in, unit1[rows], scale1[rows], norm1_gain)
        resid_grad = jnp.concatenate(resid_grads[index * 2 : index * 2 + 2], 0)
        in_grads.append((resid_grad + pulled).astype(BF16))
        return in_grads[-1]

    gate = norm1_pull(0, gate)
    gate = out_sum.over_z(gate, key_sum.near)
    gate = key_sum.over_x(gate)
    gate = value_sum.over_cores(gate)
    gate = query_sum.over_z(gate, value_sum.near)
    gate = value_sum.over_x(gate)
    gate = norm1_pull(1, gate)
    in_grad = jnp.concatenate(in_grads, 0)

    def blocks(vector, lead):
        return jnp.transpose(vector.reshape(lead, dps, -1), (1, 0, 2)).reshape(dps, -1)

    small = jnp.concatenate(
        [
            blocks(norm1_gain_grad, 1),
            blocks(norm1_bias_grad, 1),
            blocks(query_bias_grad, heads_local),
            blocks(value_bias_grad, heads_local),
            blocks(out_bias_grad, 1),
            blocks(norm2_gain_grad, 1),
            blocks(norm2_bias_grad, 1),
            blocks(up_bias_grad, up_bias.shape[0]),
            blocks(down_bias_grad, 1),
        ],
        1,
    )
    small = small.reshape(zs, xs, cs, -1)

    def fold(field, axis, at, dim):
        def take(index):
            return lax.dynamic_index_in_dim(field, index, dim, keepdims=False)

        return take(at) + swap(take(1 - at), axis)

    small = fold(small, "c", at_c, 2)
    small = fold(small, "x", at_x, 1)
    at_z, span = lax.axis_index("z"), zs
    while span > 1:
        span //= 2
        halved = small.reshape(2, span, -1)
        side = (at_z // span) % 2
        pairs = [(i, i ^ span) for i in range(zs)]
        mine = lax.dynamic_index_in_dim(halved, side, 0, keepdims=False)
        other = lax.dynamic_index_in_dim(halved, 1 - side, 0, keepdims=False)
        small = mine + lax.ppermute(other, "z", pairs)
    small = small.reshape(-1)

    gate = key_sum.over_z(gate)
    gate = value_sum.over_z(gate)
    down_weight_grad = jnp.concatenate([item.result for item in downs], 0)
    up_weight_grad = jnp.concatenate([item.result for item in ups], 1)

    thin = head_dim // dps
    sizes = [wide, wide, heads_local * thin, heads_local * thin, wide, wide, wide]
    sizes += [up_bias.shape[0] * thin, wide]
    split, begin = [], 0
    for size in sizes:
        split.append(small[begin : begin + size])
        begin += size
    gain1, bias1, query_b, value_b, out_b, gain2, bias2, up_b, down_b = split
    return (
        outputs,
        in_grad,
        gain1,
        bias1,
        query_sum.result,
        query_b.reshape(heads_local, thin),
        key_sum.result,
        value_sum.result,
        value_b.reshape(heads_local, thin),
        out_sum.result,
        out_b,
        gain2,
        bias2,
        up_weight_grad,
        up_b.reshape(-1, thin),
        down_weight_grad,
        down_b,
    )


def solution(mesh):
    dps = mesh.shape["dp"]
    fine = Mesh(mesh.devices.reshape(dps // 4, 2, 2, mesh.shape["mp"]), ("z", "x", "c", "mp"))
    dp = ("z", "x", "c")
    in_specs = (
        P(dp, None),
        P(dp),
        P(),
        P(),
        P(None, "mp"),
        P("mp", None),
        P(None, "mp"),
        P(None, "mp"),
        P("mp", None),
        P("mp", None),
        P(),
        P(),
        P(),
        P(None, "mp"),
        P("mp", None),
        P("mp", None),
        P(),
        P(dp, None),
    )
    out_specs = (
        P(dp, None),
        P(dp, None),
        P(dp),
        P(dp),
        P(dp, "mp"),
        P("mp", dp),
        P(dp, "mp"),
        P(dp, "mp"),
        P("mp", dp),
        P("mp", dp),
        P(dp),
        P(dp),
        P(dp),
        P(dp, "mp"),
        P("mp", dp),
        P("mp", dp),
        P(dp),
    )
    return jax.shard_map(body, mesh=fine, in_specs=in_specs, out_specs=out_specs, check_vma=False)
```

```python
import math

import jax
import jax.numpy as jnp
from jax import lax
from jax.experimental import pallas as pl
from jax.experimental.pallas import tpu as pltpu
from jax.sharding import Mesh
from jax.sharding import PartitionSpec as P

F32 = jnp.float32
BF16 = jnp.bfloat16
CHUNKS = 4


def swap(value, axis):
    return lax.ppermute(value, axis, [(0, 1), (1, 0)])


def mm(left, right, contract):
    return lax.dot_general(left, right, (contract, ((), ())), preferred_element_type=F32)


def norm_parts(field):
    average = jnp.mean(field, -1, keepdims=True)
    centred = field - average
    variance = jnp.mean(centred * centred, -1, keepdims=True)
    scale = lax.rsqrt(variance + 1e-05)
    return centred * scale, scale


def norm_pull(grad, unit, scale, gain):
    scaled = grad * gain
    first = jnp.mean(scaled, -1, keepdims=True)
    second = jnp.mean(scaled * unit, -1, keepdims=True)
    return scale * (scaled - first - unit * second)


def after(value, *others):
    return lax.optimization_barrier((value,) + others)[0]


def blank(shape):
    return pl.pallas_call(
        lambda out_ref: None,
        out_specs=pl.BlockSpec(memory_space=pl.ANY),
        out_shape=jax.ShapeDtypeStruct(shape, F32),
    )()


def fitting(size, most):
    block = min(size, most)
    while size % block:
        block //= 2
    return block


def paired(left, right, left_at, right_at, shape, near=None, near_at=None, extra=None):
    length = left.shape[0]
    rows, cols = fitting(shape[0], 512), fitting(shape[1], 1024)
    near_at = near_at or (0, 0)
    starts = jnp.stack(
        [
            jnp.int32(left_at // rows),
            jnp.int32(right_at // cols),
            jnp.int32(near_at[0] // rows),
            jnp.int32(near_at[1] // cols),
        ]
    )

    def kernel(starts_ref, left_ref, right_ref, *rest):
        total = mm(left_ref[...], right_ref[...], ((0,), (0,)))
        for ref in rest[:-1]:
            total = total + ref[...]
        rest[-1][...] = total

    out_spec = pl.BlockSpec((rows, cols), lambda i, j, starts: (i, j))
    in_specs = [
        pl.BlockSpec((length, rows), lambda i, j, starts: (0, starts[0] + i)),
        pl.BlockSpec((length, cols), lambda i, j, starts: (0, starts[1] + j)),
    ]
    operands = [left, right]
    if near is not None:
        in_specs.append(pl.BlockSpec((rows, cols), lambda i, j, starts: (starts[2] + i, starts[3] + j)))
        operands.append(near)
    if extra is not None:
        in_specs.append(out_spec)
        operands.append(extra)
    return pl.pallas_call(
        kernel,
        grid_spec=pltpu.PrefetchScalarGridSpec(
            num_scalar_prefetch=1,
            grid=(shape[0] // rows, shape[1] // cols),
            in_specs=in_specs,
            out_specs=out_spec,
        ),
        out_shape=jax.ShapeDtypeStruct(shape, F32),
    )(starts, *operands)


def product_down(left, right):
    rows, inner = left.shape
    cols = right.shape[1]
    deep, wide = fitting(inner, 2048), fitting(cols, 512)

    def kernel(left_ref, right_ref, out_ref):
        share = mm(left_ref[...], right_ref[...], ((1,), (0,)))

        @pl.when(pl.program_id(1) == 0)
        def _():
            out_ref[...] = share

        @pl.when(pl.program_id(1) > 0)
        def _():
            out_ref[...] += share

    return pl.pallas_call(
        kernel,
        grid=(cols // wide, inner // deep),
        in_specs=[
            pl.BlockSpec((rows, deep), lambda j, k: (0, k)),
            pl.BlockSpec((deep, wide), lambda j, k: (k, j)),
        ],
        out_specs=pl.BlockSpec((rows, wide), lambda j, k: (0, j)),
        out_shape=jax.ShapeDtypeStruct((rows, cols), F32),
    )(left, right)


def product_back(pulls, weights, rows, index):
    span = pulls[0].shape[1]
    cols = weights[0].shape[0]
    wide = fitting(cols, 512)
    count = len(pulls)

    def kernel(*refs):
        total = mm(refs[0][...], refs[count][...], ((1,), (1,)))
        for at in range(1, count):
            total = total + mm(refs[at][...], refs[count + at][...], ((1,), (1,)))
        refs[-1][...] = total

    return pl.pallas_call(
        kernel,
        grid=(cols // wide,),
        in_specs=[pl.BlockSpec((rows, span), lambda j: (index, 0))] * count
        + [pl.BlockSpec((wide, span), lambda j: (j, 0))] * count,
        out_specs=pl.BlockSpec((rows, wide), lambda j: (0, j)),
        out_shape=jax.ShapeDtypeStruct((rows, cols), F32),
    )(*pulls, *weights)


def rows_of(count, begin, seen, boundary):
    rows = begin + lax.broadcasted_iota(jnp.int32, (count, seen), 0)
    cols = lax.broadcasted_iota(jnp.int32, (count, seen), 1)
    return (cols <= rows) | (cols < boundary)


def attend(queries, keys, values, boundary, block, block_rows, head_dim):
    length, span = queries.shape
    heads = span // head_dim
    tile = min(256, block_rows)
    scale = 1.0 / math.sqrt(head_dim)

    def kernel(boundary_ref, query_ref, key_ref, value_ref, mixed_ref, log_ref):
        for at in range(0, block_rows, tile):
            begin = block * block_rows + at
            seen = max(begin + tile, length // 2)
            scores = mm(query_ref[at : at + tile, :], key_ref[:seen, :], ((1,), (1,))) * scale
            scores = jnp.where(rows_of(tile, begin, seen, boundary_ref[0]), scores, -1e30)
            peak = jnp.max(scores, -1, keepdims=True)
            exps = jnp.exp(scores - peak)
            sums = jnp.sum(exps, -1, keepdims=True)
            log_ref[0, at : at + tile, :] = peak + jnp.log(sums)
            probs = (exps / sums).astype(BF16)
            mixed = mm(probs, value_ref[:seen, :], ((1,), (0,)))
            mixed_ref[at : at + tile, :] = mixed.astype(BF16)

    whole = pl.BlockSpec((length, head_dim), lambda head: (0, head))
    return pl.pallas_call(
        kernel,
        grid=(heads,),
        in_specs=[
            pl.BlockSpec(memory_space=pltpu.SMEM),
            pl.BlockSpec((block_rows, head_dim), lambda head: (block, head)),
            whole,
            whole,
        ],
        out_specs=[
            pl.BlockSpec((block_rows, head_dim), lambda head: (0, head)),
            pl.BlockSpec((1, block_rows, 1), lambda head: (head, 0, 0)),
        ],
        out_shape=[
            jax.ShapeDtypeStruct((block_rows, span), BF16),
            jax.ShapeDtypeStruct((heads, block_rows, 1), F32),
        ],
    )(boundary, queries, keys, values)


def attend_pull(queries, keys, values, mixed_grad, totals_log, boundary, head_dim):
    length, span = queries.shape
    heads = span // head_dim
    block_rows = totals_log[0].shape[1]
    tile = min(256, block_rows)
    scale = 1.0 / math.sqrt(head_dim)
    blocks = len(totals_log)

    def kernel(boundary_ref, query_ref, key_ref, value_ref, mixed_ref, *rest):
        log_refs, (dq_ref, dk_ref, dv_ref, qb_ref, vb_ref, dk_acc, dv_acc) = rest[:blocks], rest[blocks:]
        dk_acc[...] = jnp.zeros_like(dk_acc)
        dv_acc[...] = jnp.zeros_like(dv_acc)
        query_sum = jnp.zeros((1, head_dim), F32)
        for begin in range(0, length, tile):
            seen = max(begin + tile, length // 2)
            rows = slice(begin, begin + tile)
            query = query_ref[rows, :]
            mixed = mixed_ref[rows, :]
            inner = begin % block_rows
            log_total = log_refs[begin // block_rows][0, inner : inner + tile, :]
            scores = mm(query, key_ref[:seen, :], ((1,), (1,))) * scale
            scores = jnp.where(rows_of(tile, begin, seen, boundary_ref[0]), scores, -1e30)
            probs = jnp.exp(scores - log_total)
            prob_grad = mm(mixed, value_ref[:seen, :], ((1,), (1,)))
            row_dot = jnp.sum(probs * prob_grad, -1, keepdims=True)
            score_grad = (probs * (prob_grad - row_dot) * scale).astype(BF16)
            query_grad = mm(score_grad, key_ref[:seen, :], ((1,), (0,))).astype(BF16)
            dq_ref[rows, :] = query_grad
            query_sum = query_sum + jnp.sum(query_grad.astype(F32), 0, keepdims=True)
            dk_acc[:seen, :] += mm(score_grad, query, ((0,), (0,)))
            dv_acc[:seen, :] += mm(probs.astype(BF16), mixed, ((0,), (0,)))
        dk_ref[...] = dk_acc[...].astype(BF16)
        value_grad = dv_acc[...].astype(BF16)
        dv_ref[...] = value_grad
        qb_ref[0] = query_sum
        vb_ref[0] = jnp.sum(value_grad.astype(F32), 0, keepdims=True)

    whole = pl.BlockSpec((length, head_dim), lambda head: (0, head))
    line = pl.BlockSpec((1, 1, head_dim), lambda head: (head, 0, 0))
    return pl.pallas_call(
        kernel,
        grid=(heads,),
        in_specs=[pl.BlockSpec(memory_space=pltpu.SMEM)]
        + [whole] * 4
        + [pl.BlockSpec((1, block_rows, 1), lambda head: (head, 0, 0))] * blocks,
        out_specs=[whole] * 3 + [line] * 2,
        out_shape=[jax.ShapeDtypeStruct((length, span), BF16)] * 3
        + [jax.ShapeDtypeStruct((heads, 1, head_dim), F32)] * 2,
        scratch_shapes=[pltpu.VMEM((length, head_dim), F32)] * 2,
    )(boundary, queries, keys, values, mixed_grad, *totals_log)


def hidden_step(normed2, dy, up_weight, up_bias, down_weight, index, count, kept):
    chunk, width = normed2.shape
    local = up_weight.shape[1]
    block = min(512, local)
    pair = index % 2

    def kernel(normed_ref, dy_ref, up_ref, bias_ref, down_ref, *rest):
        act_ref, pull_ref, norm_ref, sum_ref = rest[-4:]
        hidden = mm(normed_ref[...], up_ref[...], ((1,), (0,))) + bias_ref[...]
        acts_grad = mm(dy_ref[...], down_ref[...], ((1,), (1,)))
        half = 0.5 * (1.0 + lax.erf(hidden * math.sqrt(0.5)))
        act_ref[...] = (hidden * half).astype(BF16)
        slope = half + hidden * (jnp.exp(-0.5 * hidden * hidden) * (1.0 / math.sqrt(2.0 * math.pi)))
        pull = (acts_grad * slope).astype(BF16)
        pull_ref[...] = pull
        sum_ref[...] = jnp.sum(pull.astype(F32), 0, keepdims=True)
        share = mm(pull, up_ref[...], ((1,), (1,)))

        @pl.when(pl.program_id(0) == 0)
        def _():
            norm_ref[...] = share

        @pl.when(pl.program_id(0) > 0)
        def _():
            norm_ref[...] += share

    same = pl.BlockSpec((chunk, width), lambda at: (0, 0))
    wide = pl.BlockSpec((chunk, block), lambda at: (index, at))
    line = pl.BlockSpec((1, block), lambda at: (0, at))
    held = [] if kept is None else [kept[0], kept[1]] + ([kept[2]] if pair else [])
    return pl.pallas_call(
        kernel,
        grid=(local // block,),
        in_specs=[
            same,
            pl.BlockSpec((chunk, width), lambda at: (index, 0)),
            pl.BlockSpec((width, block), lambda at: (0, at)),
            line,
            pl.BlockSpec((block, width), lambda at: (at, 0)),
        ]
        + [pl.BlockSpec(memory_space=pl.ANY)] * len(held),
        out_specs=[wide, wide, pl.BlockSpec((chunk, width), lambda at: (pair, 0)), line],
        out_shape=[
            jax.ShapeDtypeStruct((chunk * count, local), BF16),
            jax.ShapeDtypeStruct((chunk * count, local), BF16),
            jax.ShapeDtypeStruct((2 * chunk, width), F32),
            jax.ShapeDtypeStruct((1, local), F32),
        ],
        input_output_aliases={5 + at: at for at in range(len(held))},
    )(normed2, dy, up_weight, up_bias, down_weight, *held)


def body(
    inputs,
    prefix_len,
    norm1_gain,
    norm1_bias,
    query_weight,
    query_bias,
    key_weight,
    value_weight,
    value_bias,
    out_weight,
    out_bias,
    norm2_gain,
    norm2_bias,
    up_weight,
    up_bias,
    down_weight,
    down_bias,
    out_grad,
):
    length, width = inputs.shape
    heads_local, head_dim = query_bias.shape
    zs, xs, cs = lax.axis_size("z"), lax.axis_size("x"), lax.axis_size("c")
    dps = zs * xs * cs
    at_x, at_c = lax.axis_index("x"), lax.axis_index("c")
    wide = width // dps
    part = zs * wide
    block_rows = min(512, length)
    block_count = length // block_rows
    chunk = length // CHUNKS

    def pieces(field, by_z=False):
        if wide % 128:
            parts = field.reshape(length, zs, xs, cs, wide)
            return jnp.transpose(parts, (0, 3, 1, 2, 4) if by_z else (0, 3, 2, 1, 4)).reshape(field.shape)

        def source(at):
            c, rest = at // (xs * zs), at % (xs * zs)
            if by_z:
                return (0, rest * cs + c)
            return (0, ((rest % zs) * xs + rest // zs) * cs + c)

        def kernel(field_ref, out_ref):
            out_ref[...] = field_ref[...]

        return pl.pallas_call(
            kernel,
            grid=(dps,),
            in_specs=[pl.BlockSpec((length, wide), source)],
            out_specs=pl.BlockSpec((length, wide), lambda at: (0, at)),
            out_shape=jax.ShapeDtypeStruct(field.shape, field.dtype),
        )(field)

    once = jnp.minimum(prefix_len[0], 1)

    def swap_now(value):
        def step(state):
            return (state[0] + 1, state[1], swap(after(state[1], state[0]), "c"))

        start = (jnp.int32(0), value, blank(value.shape))
        return lax.while_loop(lambda state: state[0] < once, step, start)[2]

    class Sum:
        def __init__(self, parts, other, by_rows, begin=0, size=None):
            self.parts, self.other, self.by_rows = parts, other, by_rows
            self.dim = 0 if by_rows else 1
            self.begin = begin
            self.size = size or other.shape[1]

        def product(self, begin, size, gate, near_at=None, extra=None):
            other = after(self.other, *gate)
            near = None if near_at is None else self.near
            if self.by_rows:
                at = None if near_at is None else (near_at, 0)
                return paired(self.parts, other, begin, self.begin, (size, self.size), near, at, extra)
            at = None if near_at is None else (0, near_at)
            return paired(other, self.parts, self.begin, begin, (self.size, size), near, at, extra)

        def over_cores(self, *gate):
            own = self.product((1 - at_c) * xs * part, xs * part, gate)
            self.own = own
            return own

        def meet(self, *gate):
            self.near = swap_now(after(self.own, *gate))
            return self.near

        def over_x(self, *gate):
            far = 1 - at_x
            own = self.product((at_c * xs + far) * part, part, gate, far * part)
            self.across = swap(own, "x")
            return own

        def over_z(self, *gate):
            across = after(self.across, *gate)
            total = self.product((at_c * xs + at_x) * part, part, gate, at_x * part, across)
            self.result = lax.psum_scatter(total, "z", scatter_dimension=self.dim, tiled=True)
            return total

        def over_z_first(self, *gate):
            total = self.product(at_c * xs * part, xs * part, gate, 0)
            self.both = lax.psum_scatter(total, "z", scatter_dimension=self.dim, tiled=True)
            return total

        def over_x_last(self, *gate):
            both = after(self.both, *gate)

            def take(x):
                return lax.dynamic_slice_in_dim(both, x * wide, wide, self.dim)

            self.result = take(at_x) + swap(take(1 - at_x), "x")
            return self.result

    features = inputs.astype(F32)
    unit1, scale1 = norm_parts(features)
    normed = (unit1 * norm1_gain + norm1_bias).astype(BF16)
    queries = (mm(normed, query_weight, ((1,), (0,))) + query_bias.reshape(-1)).astype(BF16)
    keys = mm(normed, key_weight, ((1,), (0,))).astype(BF16)
    values = (mm(normed, value_weight, ((1,), (0,))) + value_bias.reshape(-1)).astype(BF16)
    totals_log, attn_parts, mixed_blocks = [], [], []
    for block in range(block_count):
        mixed_block, log_total = attend(queries, keys, values, prefix_len, block, block_rows, head_dim)
        totals_log.append(log_total)
        mixed_blocks.append(mixed_block)
        for begin in range(0, block_rows, chunk):
            attn_parts.append(mm(mixed_block[begin : begin + chunk], out_weight, ((1,), (0,))))
    mixed = jnp.concatenate(mixed_blocks, 0)
    attn_others = [swap(piece, "mp") for piece in attn_parts]

    resids, units2, scales2, normeds2 = [], [], [], []
    shares, pull_sums, kept = [], [], None
    for index in range(CHUNKS):
        rows = slice(index * chunk, (index + 1) * chunk)
        attn_other = attn_others[index]
        if index == 0:
            attn_other = after(attn_other, attn_parts[-1])
        else:
            attn_other = after(attn_other, pull_sums[-1])
        resid = features[rows] + ((attn_parts[index] + attn_other) + out_bias)
        unit2, scale2 = norm_parts(resid)
        normed2 = (unit2 * norm2_gain + norm2_bias).astype(BF16)
        kept = hidden_step(
            normed2, out_grad, up_weight, up_bias.reshape(1, -1), down_weight, index, CHUNKS, kept
        )
        if index % 2:
            shares.append(kept[2])
        pull_sums.append(kept[3])
        resids.append(resid)
        units2.append(unit2)
        scales2.append(scale2)
        normeds2.append(normed2)
    acts, hidden_grads = kept[0], kept[1]
    up_bias_grad = sum(pull_sums)[0]
    share_others = [swap(after(shares[0], attn_others[-1]), "mp")]
    share_others.append(swap(shares[1], "mp"))

    grad_float = out_grad.astype(F32)
    down_bias_grad = jnp.sum(grad_float, 0)
    half = up_weight.shape[1] // 2
    normed2_pieces = pieces(jnp.concatenate(normeds2, 0))
    downs = [
        Sum(pieces(out_grad, begin == 0), acts, False, begin, half) for begin in (0, half)
    ]
    ups = [Sum(normed2_pieces, hidden_grads, True, begin, half) for begin in (0, half)]

    resid_grads, attn_grads, mixed_grads = [], [], []
    norm2_gain_grad, norm2_bias_grad, out_bias_grad = 0.0, 0.0, 0.0

    def norm2_pull(pair, *gate):
        nonlocal norm2_gain_grad, norm2_bias_grad, out_bias_grad
        rows = slice(pair * 2 * chunk, (pair + 1) * 2 * chunk)
        unit2 = jnp.concatenate(units2[2 * pair : 2 * pair + 2], 0)
        scale2 = jnp.concatenate(scales2[2 * pair : 2 * pair + 2], 0)
        norm2_in = shares[pair] + after(share_others[pair], *gate)
        norm2_bias_grad = norm2_bias_grad + jnp.sum(norm2_in, 0)
        norm2_gain_grad = norm2_gain_grad + jnp.sum(norm2_in * unit2, 0)
        resid_grad = grad_float[rows] + norm_pull(norm2_in, unit2, scale2, norm2_gain)
        attn_grad = resid_grad.astype(BF16)
        out_bias_grad = out_bias_grad + jnp.sum(attn_grad.astype(F32), 0)
        mixed_grads.append(mm(attn_grad, out_weight, ((1,), (1,))).astype(BF16))
        resid_grads.append(resid_grad)
        attn_grads.append(attn_grad)
        return mixed_grads[-1]

    gate = downs[0].over_cores(kept[3])
    gate = downs[0].meet(gate)
    gate = downs[0].over_z_first(gate)
    gate = downs[1].over_cores(gate)
    branch = product_down(after(acts, gate), down_weight)
    gate = downs[1].meet(branch, share_others[0])
    gate = downs[1].over_x(gate)
    gate = norm2_pull(0, gate)
    gate = ups[0].over_cores(gate)
    gate = ups[1].over_cores(gate)
    gate = norm2_pull(1, gate)
    branch_other = swap(after(branch, share_others[-1]), "mp")
    gate = downs[1].over_z(gate)
    gate = ups[0].meet(gate)
    gate = ups[0].over_x(gate)
    gate = ups[1].meet(gate)
    mixed_grad = jnp.concatenate(mixed_grads, 0)
    attn_grad = jnp.concatenate(attn_grads, 0)
    query_grad, key_grad, value_grad, query_bias_grad, value_bias_grad = attend_pull(
        queries, keys, values, after(mixed_grad, gate), totals_log, prefix_len, head_dim
    )
    gate = query_bias_grad

    half_rows = length // 2
    norm1_parts = []
    pulls = [after(query_grad, gate), key_grad, value_grad]
    for index in range(2):
        norm1_parts.append(product_back(pulls, [query_weight, key_weight, value_weight], half_rows, index))
    norm1_others = [swap(piece, "mp") for piece in norm1_parts]

    normed_pieces = pieces(normed)
    out_sum = Sum(pieces(attn_grad), mixed, False)
    query_sum, key_sum, value_sum = [
        Sum(normed_pieces, pull, True) for pull in (query_grad, key_grad, value_grad)
    ]
    gate = ups[1].over_x(*norm1_parts)
    sums = [out_sum, query_sum, key_sum, value_sum]
    for item in sums:
        gate = item.over_cores(gate)
    for item in sums:
        gate = item.meet(gate)
    gate = ups[0].over_z(gate)
    gate = out_sum.over_x(gate)
    outputs = (jnp.concatenate(resids, 0) + ((branch + after(branch_other, gate)) + down_bias)).astype(BF16)
    gate = ups[1].over_z(outputs)
    gate = query_sum.over_x(gate)
    gate = out_sum.over_z(gate)
    gate = key_sum.over_x(gate)

    norm1_gain_grad, norm1_bias_grad = 0.0, 0.0
    in_grads = []

    def norm1_pull(index, gate):
        nonlocal norm1_gain_grad, norm1_bias_grad
        rows = slice(index * half_rows, (index + 1) * half_rows)
        norm1_in = norm1_parts[index] + after(norm1_others[index], gate)
        norm1_bias_grad = norm1_bias_grad + jnp.sum(norm1_in, 0)
        norm1_gain_grad = norm1_gain_grad + jnp.sum(norm1_in * unit1[rows], 0)
        pulled = norm_pull(norm1_in, unit1[rows], scale1[rows], norm1_gain)
        in_grads.append((resid_grads[index] + pulled).astype(BF16))
        return in_grads[-1]

    gate = norm1_pull(0, gate)
    gate = query_sum.over_z(gate)
    gate = value_sum.over_x(gate)
    gate = downs[0].over_x_last(gate)
    gate = key_sum.over_z(gate)
    gate = norm1_pull(1, gate)
    in_grad = jnp.concatenate(in_grads, 0)

    def blocks(vector, lead):
        return jnp.transpose(vector.reshape(lead, dps, -1), (1, 0, 2)).reshape(dps, -1)

    small = jnp.concatenate(
        [
            blocks(norm1_gain_grad, 1),
            blocks(norm1_bias_grad, 1),
            blocks(query_bias_grad, heads_local),
            blocks(value_bias_grad, heads_local),
            blocks(out_bias_grad, 1),
            blocks(norm2_gain_grad, 1),
            blocks(norm2_bias_grad, 1),
            blocks(up_bias_grad, up_bias.shape[0]),
            blocks(down_bias_grad, 1),
        ],
        1,
    )
    small = small.reshape(zs, xs, cs, -1)

    def fold(field, axis, at, dim):
        def take(index):
            return lax.dynamic_index_in_dim(field, index, dim, keepdims=False)

        return take(at) + swap(take(1 - at), axis)

    small = fold(small, "c", at_c, 2)
    small = fold(small, "x", at_x, 1)
    at_z, span = lax.axis_index("z"), zs
    while span > 1:
        span //= 2
        halved = small.reshape(2, span, -1)
        side = (at_z // span) % 2
        pairs = [(i, i ^ span) for i in range(zs)]
        mine = lax.dynamic_index_in_dim(halved, side, 0, keepdims=False)
        other = lax.dynamic_index_in_dim(halved, 1 - side, 0, keepdims=False)
        small = mine + lax.ppermute(other, "z", pairs)
    small = small.reshape(-1)

    gate = value_sum.over_z(gate)
    down_weight_grad = jnp.concatenate([item.result for item in downs], 0)
    up_weight_grad = jnp.concatenate([item.result for item in ups], 1)

    thin = head_dim // dps
    sizes = [wide, wide, heads_local * thin, heads_local * thin, wide, wide, wide]
    sizes += [up_bias.shape[0] * thin, wide]
    split, begin = [], 0
    for size in sizes:
        split.append(small[begin : begin + size])
        begin += size
    gain1, bias1, query_b, value_b, out_b, gain2, bias2, up_b, down_b = split
    return (
        outputs,
        in_grad,
        gain1,
        bias1,
        query_sum.result,
        query_b.reshape(heads_local, thin),
        key_sum.result,
        value_sum.result,
        value_b.reshape(heads_local, thin),
        out_sum.result,
        out_b,
        gain2,
        bias2,
        up_weight_grad,
        up_b.reshape(-1, thin),
        down_weight_grad,
        down_b,
    )


def solution(mesh):
    dps = mesh.shape["dp"]
    fine = Mesh(mesh.devices.reshape(dps // 4, 2, 2, mesh.shape["mp"]), ("z", "x", "c", "mp"))
    dp = ("z", "x", "c")
    in_specs = (
        P(dp, None),
        P(dp),
        P(),
        P(),
        P(None, "mp"),
        P("mp", None),
        P(None, "mp"),
        P(None, "mp"),
        P("mp", None),
        P("mp", None),
        P(),
        P(),
        P(),
        P(None, "mp"),
        P("mp", None),
        P("mp", None),
        P(),
        P(dp, None),
    )
    out_specs = (
        P(dp, None),
        P(dp, None),
        P(dp),
        P(dp),
        P(dp, "mp"),
        P("mp", dp),
        P(dp, "mp"),
        P(dp, "mp"),
        P("mp", dp),
        P("mp", dp),
        P(dp),
        P(dp),
        P(dp),
        P(dp, "mp"),
        P("mp", dp),
        P("mp", dp),
        P(dp),
    )
    return jax.shard_map(body, mesh=fine, in_specs=in_specs, out_specs=out_specs, check_vma=False)
```

```python
import math

import jax
import jax.numpy as jnp
from jax import lax
from jax.experimental import pallas as pl
from jax.experimental.pallas import tpu as pltpu
from jax.sharding import Mesh
from jax.sharding import PartitionSpec as P

F32 = jnp.float32
BF16 = jnp.bfloat16
CHUNKS = 4


def swap(value, axis):
    return lax.ppermute(value, axis, [(0, 1), (1, 0)])


def mm(left, right, contract):
    return lax.dot_general(left, right, (contract, ((), ())), preferred_element_type=F32)


def norm_parts(field):
    average = jnp.mean(field, -1, keepdims=True)
    centred = field - average
    variance = jnp.mean(centred * centred, -1, keepdims=True)
    scale = lax.rsqrt(variance + 1e-05)
    return centred * scale, scale


def norm_pull(grad, unit, scale, gain):
    scaled = grad * gain
    first = jnp.mean(scaled, -1, keepdims=True)
    second = jnp.mean(scaled * unit, -1, keepdims=True)
    return scale * (scaled - first - unit * second)


def after(value, *others):
    return lax.optimization_barrier((value,) + others)[0]


def blank(shape):
    return pl.pallas_call(
        lambda out_ref: None,
        out_specs=pl.BlockSpec(memory_space=pl.ANY),
        out_shape=jax.ShapeDtypeStruct(shape, F32),
    )()


def fitting(size, most):
    block = min(size, most)
    while size % block:
        block //= 2
    return block


def paired(left, right, left_at, right_at, shape, near=None, near_at=None, extra=None):
    length = left.shape[0]
    rows, cols = fitting(shape[0], 512), fitting(shape[1], 1024)
    near_at = near_at or (0, 0)
    starts = jnp.stack(
        [
            jnp.int32(left_at // rows),
            jnp.int32(right_at // cols),
            jnp.int32(near_at[0] // rows),
            jnp.int32(near_at[1] // cols),
        ]
    )

    def kernel(starts_ref, left_ref, right_ref, *rest):
        total = mm(left_ref[...], right_ref[...], ((0,), (0,)))
        for ref in rest[:-1]:
            total = total + ref[...]
        rest[-1][...] = total

    out_spec = pl.BlockSpec((rows, cols), lambda i, j, starts: (i, j))
    in_specs = [
        pl.BlockSpec((length, rows), lambda i, j, starts: (0, starts[0] + i)),
        pl.BlockSpec((length, cols), lambda i, j, starts: (0, starts[1] + j)),
    ]
    operands = [left, right]
    if near is not None:
        in_specs.append(pl.BlockSpec((rows, cols), lambda i, j, starts: (starts[2] + i, starts[3] + j)))
        operands.append(near)
    if extra is not None:
        in_specs.append(out_spec)
        operands.append(extra)
    return pl.pallas_call(
        kernel,
        grid_spec=pltpu.PrefetchScalarGridSpec(
            num_scalar_prefetch=1,
            grid=(shape[0] // rows, shape[1] // cols),
            in_specs=in_specs,
            out_specs=out_spec,
        ),
        out_shape=jax.ShapeDtypeStruct(shape, F32),
    )(starts, *operands)


def product_down(left, right):
    rows, inner = left.shape
    cols = right.shape[1]
    deep, wide = fitting(inner, 2048), fitting(cols, 512)

    def kernel(left_ref, right_ref, out_ref):
        share = mm(left_ref[...], right_ref[...], ((1,), (0,)))

        @pl.when(pl.program_id(1) == 0)
        def _():
            out_ref[...] = share

        @pl.when(pl.program_id(1) > 0)
        def _():
            out_ref[...] += share

    return pl.pallas_call(
        kernel,
        grid=(cols // wide, inner // deep),
        in_specs=[
            pl.BlockSpec((rows, deep), lambda j, k: (0, k)),
            pl.BlockSpec((deep, wide), lambda j, k: (k, j)),
        ],
        out_specs=pl.BlockSpec((rows, wide), lambda j, k: (0, j)),
        out_shape=jax.ShapeDtypeStruct((rows, cols), F32),
    )(left, right)


def product_back(pulls, weights, rows, index):
    span = pulls[0].shape[1]
    cols = weights[0].shape[0]
    wide = fitting(cols, 512)
    count = len(pulls)

    def kernel(*refs):
        total = mm(refs[0][...], refs[count][...], ((1,), (1,)))
        for at in range(1, count):
            total = total + mm(refs[at][...], refs[count + at][...], ((1,), (1,)))
        refs[-1][...] = total

    return pl.pallas_call(
        kernel,
        grid=(cols // wide,),
        in_specs=[pl.BlockSpec((rows, span), lambda j: (index, 0))] * count
        + [pl.BlockSpec((wide, span), lambda j: (j, 0))] * count,
        out_specs=pl.BlockSpec((rows, wide), lambda j: (0, j)),
        out_shape=jax.ShapeDtypeStruct((rows, cols), F32),
    )(*pulls, *weights)


def rows_of(count, begin, seen, boundary):
    rows = begin + lax.broadcasted_iota(jnp.int32, (count, seen), 0)
    cols = lax.broadcasted_iota(jnp.int32, (count, seen), 1)
    return (cols <= rows) | (cols < boundary)


def attend(queries, keys, values, boundary, block, block_rows, head_dim):
    length, span = queries.shape
    heads = span // head_dim
    tile = min(256, block_rows)
    scale = 1.0 / math.sqrt(head_dim)

    def kernel(boundary_ref, query_ref, key_ref, value_ref, mixed_ref, log_ref):
        for at in range(0, block_rows, tile):
            begin = block * block_rows + at
            seen = max(begin + tile, length // 2)
            scores = mm(query_ref[at : at + tile, :], key_ref[:seen, :], ((1,), (1,))) * scale
            scores = jnp.where(rows_of(tile, begin, seen, boundary_ref[0]), scores, -1e30)
            peak = jnp.max(scores, -1, keepdims=True)
            exps = jnp.exp(scores - peak)
            sums = jnp.sum(exps, -1, keepdims=True)
            log_ref[0, at : at + tile, :] = peak + jnp.log(sums)
            probs = (exps / sums).astype(BF16)
            mixed = mm(probs, value_ref[:seen, :], ((1,), (0,)))
            mixed_ref[at : at + tile, :] = mixed.astype(BF16)

    whole = pl.BlockSpec((length, head_dim), lambda head: (0, head))
    return pl.pallas_call(
        kernel,
        grid=(heads,),
        in_specs=[
            pl.BlockSpec(memory_space=pltpu.SMEM),
            pl.BlockSpec((block_rows, head_dim), lambda head: (block, head)),
            whole,
            whole,
        ],
        out_specs=[
            pl.BlockSpec((block_rows, head_dim), lambda head: (0, head)),
            pl.BlockSpec((1, block_rows, 1), lambda head: (head, 0, 0)),
        ],
        out_shape=[
            jax.ShapeDtypeStruct((block_rows, span), BF16),
            jax.ShapeDtypeStruct((heads, block_rows, 1), F32),
        ],
    )(boundary, queries, keys, values)


def attend_pull(queries, keys, values, mixed_grad, totals_log, boundary, head_dim):
    length, span = queries.shape
    heads = span // head_dim
    block_rows = totals_log[0].shape[1]
    tile = min(256, block_rows)
    scale = 1.0 / math.sqrt(head_dim)
    blocks = len(totals_log)

    def kernel(boundary_ref, query_ref, key_ref, value_ref, mixed_ref, *rest):
        log_refs, (dq_ref, dk_ref, dv_ref, qb_ref, vb_ref, dk_acc, dv_acc) = rest[:blocks], rest[blocks:]
        dk_acc[...] = jnp.zeros_like(dk_acc)
        dv_acc[...] = jnp.zeros_like(dv_acc)
        query_sum = jnp.zeros((1, head_dim), F32)
        for begin in range(0, length, tile):
            seen = max(begin + tile, length // 2)
            rows = slice(begin, begin + tile)
            query = query_ref[rows, :]
            mixed = mixed_ref[rows, :]
            inner = begin % block_rows
            log_total = log_refs[begin // block_rows][0, inner : inner + tile, :]
            scores = mm(query, key_ref[:seen, :], ((1,), (1,))) * scale
            scores = jnp.where(rows_of(tile, begin, seen, boundary_ref[0]), scores, -1e30)
            probs = jnp.exp(scores - log_total)
            prob_grad = mm(mixed, value_ref[:seen, :], ((1,), (1,)))
            row_dot = jnp.sum(probs * prob_grad, -1, keepdims=True)
            score_grad = (probs * (prob_grad - row_dot) * scale).astype(BF16)
            query_grad = mm(score_grad, key_ref[:seen, :], ((1,), (0,))).astype(BF16)
            dq_ref[rows, :] = query_grad
            query_sum = query_sum + jnp.sum(query_grad.astype(F32), 0, keepdims=True)
            dk_acc[:seen, :] += mm(score_grad, query, ((0,), (0,)))
            dv_acc[:seen, :] += mm(probs.astype(BF16), mixed, ((0,), (0,)))
        dk_ref[...] = dk_acc[...].astype(BF16)
        value_grad = dv_acc[...].astype(BF16)
        dv_ref[...] = value_grad
        qb_ref[0] = query_sum
        vb_ref[0] = jnp.sum(value_grad.astype(F32), 0, keepdims=True)

    whole = pl.BlockSpec((length, head_dim), lambda head: (0, head))
    line = pl.BlockSpec((1, 1, head_dim), lambda head: (head, 0, 0))
    return pl.pallas_call(
        kernel,
        grid=(heads,),
        in_specs=[pl.BlockSpec(memory_space=pltpu.SMEM)]
        + [whole] * 4
        + [pl.BlockSpec((1, block_rows, 1), lambda head: (head, 0, 0))] * blocks,
        out_specs=[whole] * 3 + [line] * 2,
        out_shape=[jax.ShapeDtypeStruct((length, span), BF16)] * 3
        + [jax.ShapeDtypeStruct((heads, 1, head_dim), F32)] * 2,
        scratch_shapes=[pltpu.VMEM((length, head_dim), F32)] * 2,
    )(boundary, queries, keys, values, mixed_grad, *totals_log)


def hidden_step(normed2, dy, up_weight, up_bias, down_weight, index, count, kept):
    chunk, width = normed2.shape
    local = up_weight.shape[1]
    block = min(512, local)
    pair = index % 2

    def kernel(normed_ref, dy_ref, up_ref, bias_ref, down_ref, *rest):
        act_ref, pull_ref, norm_ref, sum_ref = rest[-4:]
        hidden = mm(normed_ref[...], up_ref[...], ((1,), (0,))) + bias_ref[...]
        acts_grad = mm(dy_ref[...], down_ref[...], ((1,), (1,)))
        half = 0.5 * (1.0 + lax.erf(hidden * math.sqrt(0.5)))
        act_ref[...] = (hidden * half).astype(BF16)
        slope = half + hidden * (jnp.exp(-0.5 * hidden * hidden) * (1.0 / math.sqrt(2.0 * math.pi)))
        pull = (acts_grad * slope).astype(BF16)
        pull_ref[...] = pull
        sum_ref[...] = jnp.sum(pull.astype(F32), 0, keepdims=True)
        share = mm(pull, up_ref[...], ((1,), (1,)))

        @pl.when(pl.program_id(0) == 0)
        def _():
            norm_ref[...] = share

        @pl.when(pl.program_id(0) > 0)
        def _():
            norm_ref[...] += share

    same = pl.BlockSpec((chunk, width), lambda at: (0, 0))
    wide = pl.BlockSpec((chunk, block), lambda at: (index, at))
    line = pl.BlockSpec((1, block), lambda at: (0, at))
    held = [] if kept is None else [kept[0], kept[1]] + ([kept[2]] if pair else [])
    return pl.pallas_call(
        kernel,
        grid=(local // block,),
        in_specs=[
            same,
            pl.BlockSpec((chunk, width), lambda at: (index, 0)),
            pl.BlockSpec((width, block), lambda at: (0, at)),
            line,
            pl.BlockSpec((block, width), lambda at: (at, 0)),
        ]
        + [pl.BlockSpec(memory_space=pl.ANY)] * len(held),
        out_specs=[wide, wide, pl.BlockSpec((chunk, width), lambda at: (pair, 0)), line],
        out_shape=[
            jax.ShapeDtypeStruct((chunk * count, local), BF16),
            jax.ShapeDtypeStruct((chunk * count, local), BF16),
            jax.ShapeDtypeStruct((2 * chunk, width), F32),
            jax.ShapeDtypeStruct((1, local), F32),
        ],
        input_output_aliases={5 + at: at for at in range(len(held))},
    )(normed2, dy, up_weight, up_bias, down_weight, *held)


def body(
    inputs,
    prefix_len,
    norm1_gain,
    norm1_bias,
    query_weight,
    query_bias,
    key_weight,
    value_weight,
    value_bias,
    out_weight,
    out_bias,
    norm2_gain,
    norm2_bias,
    up_weight,
    up_bias,
    down_weight,
    down_bias,
    out_grad,
):
    length, width = inputs.shape
    heads_local, head_dim = query_bias.shape
    zs, xs, cs = lax.axis_size("z"), lax.axis_size("x"), lax.axis_size("c")
    dps = zs * xs * cs
    at_x, at_c = lax.axis_index("x"), lax.axis_index("c")
    wide = width // dps
    part = zs * wide
    block_rows = min(512, length)
    block_count = length // block_rows
    chunk = length // CHUNKS

    def pieces(field, by_z=False):
        if wide % 128:
            parts = field.reshape(length, zs, xs, cs, wide)
            return jnp.transpose(parts, (0, 3, 1, 2, 4) if by_z else (0, 3, 2, 1, 4)).reshape(field.shape)

        def source(at):
            c, rest = at // (xs * zs), at % (xs * zs)
            if by_z:
                return (0, rest * cs + c)
            return (0, ((rest % zs) * xs + rest // zs) * cs + c)

        def kernel(field_ref, out_ref):
            out_ref[...] = field_ref[...]

        return pl.pallas_call(
            kernel,
            grid=(dps,),
            in_specs=[pl.BlockSpec((length, wide), source)],
            out_specs=pl.BlockSpec((length, wide), lambda at: (0, at)),
            out_shape=jax.ShapeDtypeStruct(field.shape, field.dtype),
        )(field)

    once = jnp.minimum(prefix_len[0], 1)

    def swap_now(value, axis):
        def step(state):
            return (state[0] + 1, state[1], swap(after(state[1], state[0]), axis))

        start = (jnp.int32(0), value, blank(value.shape))
        return lax.while_loop(lambda state: state[0] < once, step, start)[2]

    class Sum:
        def __init__(self, parts, other, by_rows, begin=0, size=None):
            self.parts, self.other, self.by_rows = parts, other, by_rows
            self.dim = 0 if by_rows else 1
            self.begin = begin
            self.size = size or other.shape[1]

        def product(self, begin, size, gate, near_at=None, extra=None):
            other = after(self.other, *gate)
            near = None if near_at is None else self.near
            if self.by_rows:
                at = None if near_at is None else (near_at, 0)
                return paired(self.parts, other, begin, self.begin, (size, self.size), near, at, extra)
            at = None if near_at is None else (0, near_at)
            return paired(other, self.parts, self.begin, begin, (self.size, size), near, at, extra)

        def over_cores(self, *gate):
            own = self.product((1 - at_c) * xs * part, xs * part, gate)
            self.own = own
            return own

        def meet(self, *gate):
            self.near = swap_now(after(self.own, *gate), "c")
            return self.near

        def over_x(self, *gate):
            far = 1 - at_x
            own = self.product((at_c * xs + far) * part, part, gate, far * part)
            self.across = swap(own, "x")
            return own

        def over_z(self, *gate):
            across = after(self.across, *gate)
            total = self.product((at_c * xs + at_x) * part, part, gate, at_x * part, across)
            self.result = lax.psum_scatter(total, "z", scatter_dimension=self.dim, tiled=True)
            return total

        def over_z_first(self, *gate):
            total = self.product(at_c * xs * part, xs * part, gate, 0)
            self.both = lax.psum_scatter(total, "z", scatter_dimension=self.dim, tiled=True)
            return total

        def over_x_last(self, *gate):
            both = after(self.both, *gate)

            def take(x):
                return lax.dynamic_slice_in_dim(both, x * wide, wide, self.dim)

            self.result = take(at_x) + swap(take(1 - at_x), "x")
            return self.result

    features = inputs.astype(F32)
    unit1, scale1 = norm_parts(features)
    normed = (unit1 * norm1_gain + norm1_bias).astype(BF16)
    queries = (mm(normed, query_weight, ((1,), (0,))) + query_bias.reshape(-1)).astype(BF16)
    keys = mm(normed, key_weight, ((1,), (0,))).astype(BF16)
    values = (mm(normed, value_weight, ((1,), (0,))) + value_bias.reshape(-1)).astype(BF16)
    totals_log, attn_parts, mixed_blocks = [], [], []
    for block in range(block_count):
        mixed_block, log_total = attend(queries, keys, values, prefix_len, block, block_rows, head_dim)
        totals_log.append(log_total)
        mixed_blocks.append(mixed_block)
        for begin in range(0, block_rows, chunk):
            attn_parts.append(mm(mixed_block[begin : begin + chunk], out_weight, ((1,), (0,))))
    mixed = jnp.concatenate(mixed_blocks, 0)
    attn_others = [swap(piece, "mp") for piece in attn_parts]

    resids, units2, scales2, normeds2 = [], [], [], []
    shares, pull_sums, kept = [], [], None
    for index in range(CHUNKS):
        rows = slice(index * chunk, (index + 1) * chunk)
        attn_other = attn_others[index]
        if index == 0:
            attn_other = after(attn_other, attn_parts[-1])
        else:
            attn_other = after(attn_other, pull_sums[-1])
        resid = features[rows] + ((attn_parts[index] + attn_other) + out_bias)
        unit2, scale2 = norm_parts(resid)
        normed2 = (unit2 * norm2_gain + norm2_bias).astype(BF16)
        kept = hidden_step(
            normed2, out_grad, up_weight, up_bias.reshape(1, -1), down_weight, index, CHUNKS, kept
        )
        if index % 2:
            shares.append(kept[2])
        pull_sums.append(kept[3])
        resids.append(resid)
        units2.append(unit2)
        scales2.append(scale2)
        normeds2.append(normed2)
    acts, hidden_grads = kept[0], kept[1]
    up_bias_grad = sum(pull_sums)[0]
    share_others = [swap(after(shares[0], attn_others[-1]), "mp")]
    share_others.append(swap(shares[1], "mp"))

    grad_float = out_grad.astype(F32)
    down_bias_grad = jnp.sum(grad_float, 0)
    half = up_weight.shape[1] // 2
    normed2_pieces = pieces(jnp.concatenate(normeds2, 0))
    downs = [
        Sum(pieces(out_grad, begin == 0), acts, False, begin, half) for begin in (0, half)
    ]
    ups = [Sum(normed2_pieces, hidden_grads, True, begin, half) for begin in (0, half)]

    resid_grads, attn_grads, mixed_grads = [], [], []
    norm2_gain_grad, norm2_bias_grad, out_bias_grad = 0.0, 0.0, 0.0

    def norm2_pull(pair, *gate):
        nonlocal norm2_gain_grad, norm2_bias_grad, out_bias_grad
        rows = slice(pair * 2 * chunk, (pair + 1) * 2 * chunk)
        unit2 = jnp.concatenate(units2[2 * pair : 2 * pair + 2], 0)
        scale2 = jnp.concatenate(scales2[2 * pair : 2 * pair + 2], 0)
        norm2_in = shares[pair] + after(share_others[pair], *gate)
        norm2_bias_grad = norm2_bias_grad + jnp.sum(norm2_in, 0)
        norm2_gain_grad = norm2_gain_grad + jnp.sum(norm2_in * unit2, 0)
        resid_grad = grad_float[rows] + norm_pull(norm2_in, unit2, scale2, norm2_gain)
        attn_grad = resid_grad.astype(BF16)
        out_bias_grad = out_bias_grad + jnp.sum(attn_grad.astype(F32), 0)
        mixed_grads.append(mm(attn_grad, out_weight, ((1,), (1,))).astype(BF16))
        resid_grads.append(resid_grad)
        attn_grads.append(attn_grad)
        return mixed_grads[-1]

    gate = downs[0].over_cores(kept[3])
    gate = downs[0].meet(gate)
    gate = downs[0].over_z_first(gate)
    gate = downs[1].over_cores(gate)
    gate = downs[1].meet(gate)
    gate = downs[1].over_x(gate)
    gate = ups[0].over_cores(gate)
    gate = ups[0].meet(gate)
    gate = ups[0].over_x(gate)
    gate = downs[1].over_z(gate, share_others[0])
    gate = norm2_pull(0, gate)
    branch = product_down(after(acts, gate), down_weight)
    gate = ups[1].over_cores(branch)
    gate = norm2_pull(1, gate)
    branch_other = swap(after(branch, share_others[-1]), "mp")
    gate = ups[1].meet(gate)
    gate = ups[1].over_x(gate)
    gate = ups[0].over_z(gate)
    mixed_grad = jnp.concatenate(mixed_grads, 0)
    attn_grad = jnp.concatenate(attn_grads, 0)
    query_grad, key_grad, value_grad, query_bias_grad, value_bias_grad = attend_pull(
        queries, keys, values, after(mixed_grad, gate), totals_log, prefix_len, head_dim
    )
    gate = query_bias_grad

    spans = [(0, 3 * length // 4), (3 * length // 4, length)]
    resid_grad = jnp.concatenate(resid_grads, 0)
    norm1_parts = []
    pulls = [after(query_grad, gate), key_grad, value_grad]
    for begin, end in spans:
        rows = end - begin
        norm1_parts.append(product_back(pulls, [query_weight, key_weight, value_weight], rows, begin // rows))
    norm1_others = [swap(piece, "mp") for piece in norm1_parts]

    normed_pieces = pieces(normed)
    out_sum = Sum(pieces(attn_grad), mixed, False)
    query_sum, key_sum, value_sum = [
        Sum(normed_pieces, pull, True) for pull in (query_grad, key_grad, value_grad)
    ]
    sums = [out_sum, query_sum, key_sum, value_sum]
    for item in sums:
        gate = item.over_cores(*norm1_parts)
    gate = sums[-1].own
    for item in sums:
        gate = item.meet(gate)
    gate = out_sum.over_x(gate)
    outputs = (jnp.concatenate(resids, 0) + ((branch + after(branch_other, gate)) + down_bias)).astype(BF16)
    gate = ups[1].over_z(outputs)
    gate = query_sum.over_x(gate)
    gate = out_sum.over_z(gate)
    gate = key_sum.over_x(gate)

    norm1_gain_grad, norm1_bias_grad = 0.0, 0.0
    in_grads = []

    def norm1_pull(index, gate):
        nonlocal norm1_gain_grad, norm1_bias_grad
        rows = slice(*spans[index])
        norm1_in = norm1_parts[index] + after(norm1_others[index], gate)
        norm1_bias_grad = norm1_bias_grad + jnp.sum(norm1_in, 0)
        norm1_gain_grad = norm1_gain_grad + jnp.sum(norm1_in * unit1[rows], 0)
        pulled = norm_pull(norm1_in, unit1[rows], scale1[rows], norm1_gain)
        in_grads.append((resid_grad[rows] + pulled).astype(BF16))
        return in_grads[-1]

    gate = query_sum.over_z(gate)
    gate = value_sum.over_x(gate)
    downs[0].over_x_last(gate)
    gate = norm1_pull(0, gate)
    gate = key_sum.over_z(gate)
    gate = norm1_pull(1, gate)
    gate = value_sum.over_z(gate)
    in_grad = jnp.concatenate(in_grads, 0)

    def blocks(vector, lead):
        return jnp.transpose(vector.reshape(lead, dps, -1), (1, 0, 2)).reshape(dps, -1)

    small = jnp.concatenate(
        [
            blocks(norm1_gain_grad, 1),
            blocks(norm1_bias_grad, 1),
            blocks(query_bias_grad, heads_local),
            blocks(value_bias_grad, heads_local),
            blocks(out_bias_grad, 1),
            blocks(norm2_gain_grad, 1),
            blocks(norm2_bias_grad, 1),
            blocks(up_bias_grad, up_bias.shape[0]),
            blocks(down_bias_grad, 1),
        ],
        1,
    )
    small = small.reshape(zs, xs, cs, -1)

    def fold(field, axis, at, dim):
        def take(index):
            return lax.dynamic_index_in_dim(field, index, dim, keepdims=False)

        return take(at) + swap(take(1 - at), axis)

    small = fold(small, "c", at_c, 2)
    small = fold(small, "x", at_x, 1)
    at_z, span = lax.axis_index("z"), zs
    while span > 1:
        span //= 2
        halved = small.reshape(2, span, -1)
        side = (at_z // span) % 2
        pairs = [(i, i ^ span) for i in range(zs)]
        mine = lax.dynamic_index_in_dim(halved, side, 0, keepdims=False)
        other = lax.dynamic_index_in_dim(halved, 1 - side, 0, keepdims=False)
        small = mine + lax.ppermute(other, "z", pairs)
    small = small.reshape(-1)

    down_weight_grad = jnp.concatenate([item.result for item in downs], 0)
    up_weight_grad = jnp.concatenate([item.result for item in ups], 1)

    thin = head_dim // dps
    sizes = [wide, wide, heads_local * thin, heads_local * thin, wide, wide, wide]
    sizes += [up_bias.shape[0] * thin, wide]
    split, begin = [], 0
    for size in sizes:
        split.append(small[begin : begin + size])
        begin += size
    gain1, bias1, query_b, value_b, out_b, gain2, bias2, up_b, down_b = split
    return (
        outputs,
        in_grad,
        gain1,
        bias1,
        query_sum.result,
        query_b.reshape(heads_local, thin),
        key_sum.result,
        value_sum.result,
        value_b.reshape(heads_local, thin),
        out_sum.result,
        out_b,
        gain2,
        bias2,
        up_weight_grad,
        up_b.reshape(-1, thin),
        down_weight_grad,
        down_b,
    )


def solution(mesh):
    dps = mesh.shape["dp"]
    fine = Mesh(mesh.devices.reshape(dps // 4, 2, 2, mesh.shape["mp"]), ("z", "x", "c", "mp"))
    dp = ("z", "x", "c")
    in_specs = (
        P(dp, None),
        P(dp),
        P(),
        P(),
        P(None, "mp"),
        P("mp", None),
        P(None, "mp"),
        P(None, "mp"),
        P("mp", None),
        P("mp", None),
        P(),
        P(),
        P(),
        P(None, "mp"),
        P("mp", None),
        P("mp", None),
        P(),
        P(dp, None),
    )
    out_specs = (
        P(dp, None),
        P(dp, None),
        P(dp),
        P(dp),
        P(dp, "mp"),
        P("mp", dp),
        P(dp, "mp"),
        P(dp, "mp"),
        P("mp", dp),
        P("mp", dp),
        P(dp),
        P(dp),
        P(dp),
        P(dp, "mp"),
        P("mp", dp),
        P("mp", dp),
        P(dp),
    )
    return jax.shard_map(body, mesh=fine, in_specs=in_specs, out_specs=out_specs, check_vma=False)
```

```python
import math

import jax
import jax.numpy as jnp
from jax import lax
from jax.experimental import pallas as pl
from jax.experimental.pallas import tpu as pltpu
from jax.sharding import Mesh
from jax.sharding import PartitionSpec as P

F32 = jnp.float32
BF16 = jnp.bfloat16
CHUNKS = 4


def swap(value, axis):
    return lax.ppermute(value, axis, [(0, 1), (1, 0)])


def mm(left, right, contract):
    return lax.dot_general(left, right, (contract, ((), ())), preferred_element_type=F32)


def norm_parts(field):
    average = jnp.mean(field, -1, keepdims=True)
    centred = field - average
    variance = jnp.mean(centred * centred, -1, keepdims=True)
    scale = lax.rsqrt(variance + 1e-05)
    return centred * scale, scale


def norm_pull(grad, unit, scale, gain):
    scaled = grad * gain
    first = jnp.mean(scaled, -1, keepdims=True)
    second = jnp.mean(scaled * unit, -1, keepdims=True)
    return scale * (scaled - first - unit * second)


def after(value, *others):
    return lax.optimization_barrier((value,) + others)[0]


def blank(shape):
    return pl.pallas_call(
        lambda out_ref: None,
        out_specs=pl.BlockSpec(memory_space=pl.ANY),
        out_shape=jax.ShapeDtypeStruct(shape, F32),
    )()


def fitting(size, most):
    block = min(size, most)
    while size % block:
        block //= 2
    return block


def paired(left, right, left_at, right_at, shape, near=None, near_at=None, extra=None):
    length = left.shape[0]
    rows, cols = fitting(shape[0], 512), fitting(shape[1], 1024)
    near_at = near_at or (0, 0)
    starts = jnp.stack(
        [
            jnp.int32(left_at // rows),
            jnp.int32(right_at // cols),
            jnp.int32(near_at[0] // rows),
            jnp.int32(near_at[1] // cols),
        ]
    )

    def kernel(starts_ref, left_ref, right_ref, *rest):
        total = mm(left_ref[...], right_ref[...], ((0,), (0,)))
        for ref in rest[:-1]:
            total = total + ref[...]
        rest[-1][...] = total

    out_spec = pl.BlockSpec((rows, cols), lambda i, j, starts: (i, j))
    in_specs = [
        pl.BlockSpec((length, rows), lambda i, j, starts: (0, starts[0] + i)),
        pl.BlockSpec((length, cols), lambda i, j, starts: (0, starts[1] + j)),
    ]
    operands = [left, right]
    if near is not None:
        in_specs.append(pl.BlockSpec((rows, cols), lambda i, j, starts: (starts[2] + i, starts[3] + j)))
        operands.append(near)
    if extra is not None:
        in_specs.append(out_spec)
        operands.append(extra)
    return pl.pallas_call(
        kernel,
        grid_spec=pltpu.PrefetchScalarGridSpec(
            num_scalar_prefetch=1,
            grid=(shape[0] // rows, shape[1] // cols),
            in_specs=in_specs,
            out_specs=out_spec,
        ),
        out_shape=jax.ShapeDtypeStruct(shape, F32),
    )(starts, *operands)


def product_down(left, right):
    rows, inner = left.shape
    cols = right.shape[1]
    deep, wide = fitting(inner, 2048), fitting(cols, 512)

    def kernel(left_ref, right_ref, out_ref):
        share = mm(left_ref[...], right_ref[...], ((1,), (0,)))

        @pl.when(pl.program_id(1) == 0)
        def _():
            out_ref[...] = share

        @pl.when(pl.program_id(1) > 0)
        def _():
            out_ref[...] += share

    return pl.pallas_call(
        kernel,
        grid=(cols // wide, inner // deep),
        in_specs=[
            pl.BlockSpec((rows, deep), lambda j, k: (0, k)),
            pl.BlockSpec((deep, wide), lambda j, k: (k, j)),
        ],
        out_specs=pl.BlockSpec((rows, wide), lambda j, k: (0, j)),
        out_shape=jax.ShapeDtypeStruct((rows, cols), F32),
    )(left, right)


def product_back(pulls, weights, rows, index):
    span = pulls[0].shape[1]
    cols = weights[0].shape[0]
    wide = fitting(cols, 512)
    count = len(pulls)

    def kernel(*refs):
        total = mm(refs[0][...], refs[count][...], ((1,), (1,)))
        for at in range(1, count):
            total = total + mm(refs[at][...], refs[count + at][...], ((1,), (1,)))
        refs[-1][...] = total

    return pl.pallas_call(
        kernel,
        grid=(cols // wide,),
        in_specs=[pl.BlockSpec((rows, span), lambda j: (index, 0))] * count
        + [pl.BlockSpec((wide, span), lambda j: (j, 0))] * count,
        out_specs=pl.BlockSpec((rows, wide), lambda j: (0, j)),
        out_shape=jax.ShapeDtypeStruct((rows, cols), F32),
    )(*pulls, *weights)


def rows_of(count, begin, seen, boundary):
    rows = begin + lax.broadcasted_iota(jnp.int32, (count, seen), 0)
    cols = lax.broadcasted_iota(jnp.int32, (count, seen), 1)
    return (cols <= rows) | (cols < boundary)


def attend(queries, keys, values, boundary, block, block_rows, head_dim):
    length, span = queries.shape
    heads = span // head_dim
    tile = min(256, block_rows)
    scale = 1.0 / math.sqrt(head_dim)

    def kernel(boundary_ref, query_ref, key_ref, value_ref, mixed_ref, log_ref):
        for at in range(0, block_rows, tile):
            begin = block * block_rows + at
            seen = max(begin + tile, length // 2)
            scores = mm(query_ref[at : at + tile, :], key_ref[:seen, :], ((1,), (1,))) * scale
            scores = jnp.where(rows_of(tile, begin, seen, boundary_ref[0]), scores, -1e30)
            peak = jnp.max(scores, -1, keepdims=True)
            exps = jnp.exp(scores - peak)
            sums = jnp.sum(exps, -1, keepdims=True)
            log_ref[0, at : at + tile, :] = peak + jnp.log(sums)
            probs = (exps / sums).astype(BF16)
            mixed = mm(probs, value_ref[:seen, :], ((1,), (0,)))
            mixed_ref[at : at + tile, :] = mixed.astype(BF16)

    whole = pl.BlockSpec((length, head_dim), lambda head: (0, head))
    return pl.pallas_call(
        kernel,
        grid=(heads,),
        in_specs=[
            pl.BlockSpec(memory_space=pltpu.SMEM),
            pl.BlockSpec((block_rows, head_dim), lambda head: (block, head)),
            whole,
            whole,
        ],
        out_specs=[
            pl.BlockSpec((block_rows, head_dim), lambda head: (0, head)),
            pl.BlockSpec((1, block_rows, 1), lambda head: (head, 0, 0)),
        ],
        out_shape=[
            jax.ShapeDtypeStruct((block_rows, span), BF16),
            jax.ShapeDtypeStruct((heads, block_rows, 1), F32),
        ],
    )(boundary, queries, keys, values)


def attend_pull(queries, keys, values, mixed_grad, totals_log, boundary, head_dim):
    length, span = queries.shape
    heads = span // head_dim
    block_rows = totals_log[0].shape[1]
    tile = min(256, block_rows)
    scale = 1.0 / math.sqrt(head_dim)
    blocks = len(totals_log)

    def kernel(boundary_ref, query_ref, key_ref, value_ref, mixed_ref, *rest):
        log_refs, (dq_ref, dk_ref, dv_ref, qb_ref, vb_ref, dk_acc, dv_acc) = rest[:blocks], rest[blocks:]
        dk_acc[...] = jnp.zeros_like(dk_acc)
        dv_acc[...] = jnp.zeros_like(dv_acc)
        query_sum = jnp.zeros((1, head_dim), F32)
        for begin in range(0, length, tile):
            seen = max(begin + tile, length // 2)
            rows = slice(begin, begin + tile)
            query = query_ref[rows, :]
            mixed = mixed_ref[rows, :]
            inner = begin % block_rows
            log_total = log_refs[begin // block_rows][0, inner : inner + tile, :]
            scores = mm(query, key_ref[:seen, :], ((1,), (1,))) * scale
            scores = jnp.where(rows_of(tile, begin, seen, boundary_ref[0]), scores, -1e30)
            probs = jnp.exp(scores - log_total)
            prob_grad = mm(mixed, value_ref[:seen, :], ((1,), (1,)))
            row_dot = jnp.sum(probs * prob_grad, -1, keepdims=True)
            score_grad = (probs * (prob_grad - row_dot) * scale).astype(BF16)
            query_grad = mm(score_grad, key_ref[:seen, :], ((1,), (0,))).astype(BF16)
            dq_ref[rows, :] = query_grad
            query_sum = query_sum + jnp.sum(query_grad.astype(F32), 0, keepdims=True)
            dk_acc[:seen, :] += mm(score_grad, query, ((0,), (0,)))
            dv_acc[:seen, :] += mm(probs.astype(BF16), mixed, ((0,), (0,)))
        dk_ref[...] = dk_acc[...].astype(BF16)
        value_grad = dv_acc[...].astype(BF16)
        dv_ref[...] = value_grad
        qb_ref[0] = query_sum
        vb_ref[0] = jnp.sum(value_grad.astype(F32), 0, keepdims=True)

    whole = pl.BlockSpec((length, head_dim), lambda head: (0, head))
    line = pl.BlockSpec((1, 1, head_dim), lambda head: (head, 0, 0))
    return pl.pallas_call(
        kernel,
        grid=(heads,),
        in_specs=[pl.BlockSpec(memory_space=pltpu.SMEM)]
        + [whole] * 4
        + [pl.BlockSpec((1, block_rows, 1), lambda head: (head, 0, 0))] * blocks,
        out_specs=[whole] * 3 + [line] * 2,
        out_shape=[jax.ShapeDtypeStruct((length, span), BF16)] * 3
        + [jax.ShapeDtypeStruct((heads, 1, head_dim), F32)] * 2,
        scratch_shapes=[pltpu.VMEM((length, head_dim), F32)] * 2,
    )(boundary, queries, keys, values, mixed_grad, *totals_log)


def hidden_step(normed2, dy, up_weight, up_bias, down_weight, index, count, kept):
    chunk, width = normed2.shape
    local = up_weight.shape[1]
    block = min(512, local)
    pair = index % 2

    def kernel(normed_ref, dy_ref, up_ref, bias_ref, down_ref, *rest):
        act_ref, pull_ref, norm_ref, sum_ref = rest[-4:]
        hidden = mm(normed_ref[...], up_ref[...], ((1,), (0,))) + bias_ref[...]
        acts_grad = mm(dy_ref[...], down_ref[...], ((1,), (1,)))
        half = 0.5 * (1.0 + lax.erf(hidden * math.sqrt(0.5)))
        act_ref[...] = (hidden * half).astype(BF16)
        slope = half + hidden * (jnp.exp(-0.5 * hidden * hidden) * (1.0 / math.sqrt(2.0 * math.pi)))
        pull = (acts_grad * slope).astype(BF16)
        pull_ref[...] = pull
        sum_ref[...] = jnp.sum(pull.astype(F32), 0, keepdims=True)
        share = mm(pull, up_ref[...], ((1,), (1,)))

        @pl.when(pl.program_id(0) == 0)
        def _():
            norm_ref[...] = share

        @pl.when(pl.program_id(0) > 0)
        def _():
            norm_ref[...] += share

    same = pl.BlockSpec((chunk, width), lambda at: (0, 0))
    wide = pl.BlockSpec((chunk, block), lambda at: (index, at))
    line = pl.BlockSpec((1, block), lambda at: (0, at))
    held = [] if kept is None else [kept[0], kept[1]] + ([kept[2]] if pair else [])
    return pl.pallas_call(
        kernel,
        grid=(local // block,),
        in_specs=[
            same,
            pl.BlockSpec((chunk, width), lambda at: (index, 0)),
            pl.BlockSpec((width, block), lambda at: (0, at)),
            line,
            pl.BlockSpec((block, width), lambda at: (at, 0)),
        ]
        + [pl.BlockSpec(memory_space=pl.ANY)] * len(held),
        out_specs=[wide, wide, pl.BlockSpec((chunk, width), lambda at: (pair, 0)), line],
        out_shape=[
            jax.ShapeDtypeStruct((chunk * count, local), BF16),
            jax.ShapeDtypeStruct((chunk * count, local), BF16),
            jax.ShapeDtypeStruct((2 * chunk, width), F32),
            jax.ShapeDtypeStruct((1, local), F32),
        ],
        input_output_aliases={5 + at: at for at in range(len(held))},
    )(normed2, dy, up_weight, up_bias, down_weight, *held)


def body(
    inputs,
    prefix_len,
    norm1_gain,
    norm1_bias,
    query_weight,
    query_bias,
    key_weight,
    value_weight,
    value_bias,
    out_weight,
    out_bias,
    norm2_gain,
    norm2_bias,
    up_weight,
    up_bias,
    down_weight,
    down_bias,
    out_grad,
):
    length, width = inputs.shape
    heads_local, head_dim = query_bias.shape
    zs, xs, cs = lax.axis_size("z"), lax.axis_size("x"), lax.axis_size("c")
    dps = zs * xs * cs
    at_x, at_c = lax.axis_index("x"), lax.axis_index("c")
    wide = width // dps
    part = zs * wide
    block_rows = min(512, length)
    block_count = length // block_rows
    chunk = length // CHUNKS

    def pieces(field, by_z=False):
        if wide % 128:
            parts = field.reshape(length, zs, xs, cs, wide)
            return jnp.transpose(parts, (0, 3, 1, 2, 4) if by_z else (0, 3, 2, 1, 4)).reshape(field.shape)

        def source(at):
            c, rest = at // (xs * zs), at % (xs * zs)
            if by_z:
                return (0, rest * cs + c)
            return (0, ((rest % zs) * xs + rest // zs) * cs + c)

        def kernel(field_ref, out_ref):
            out_ref[...] = field_ref[...]

        return pl.pallas_call(
            kernel,
            grid=(dps,),
            in_specs=[pl.BlockSpec((length, wide), source)],
            out_specs=pl.BlockSpec((length, wide), lambda at: (0, at)),
            out_shape=jax.ShapeDtypeStruct(field.shape, field.dtype),
        )(field)

    once = jnp.minimum(prefix_len[0], 1)

    def swap_now(value, axis):
        def step(state):
            return (state[0] + 1, state[1], swap(after(state[1], state[0]), axis))

        start = (jnp.int32(0), value, blank(value.shape))
        return lax.while_loop(lambda state: state[0] < once, step, start)[2]

    class Sum:
        def __init__(self, parts, other, by_rows, begin=0, size=None):
            self.parts, self.other, self.by_rows = parts, other, by_rows
            self.dim = 0 if by_rows else 1
            self.begin = begin
            self.size = size or other.shape[1]

        def product(self, begin, size, gate, near_at=None, extra=None):
            other = after(self.other, *gate)
            near = None if near_at is None else self.near
            if self.by_rows:
                at = None if near_at is None else (near_at, 0)
                return paired(self.parts, other, begin, self.begin, (size, self.size), near, at, extra)
            at = None if near_at is None else (0, near_at)
            return paired(other, self.parts, self.begin, begin, (self.size, size), near, at, extra)

        def over_cores(self, *gate):
            own = self.product((1 - at_c) * xs * part, xs * part, gate)
            self.own = own
            return own

        def meet(self, *gate):
            self.near = swap_now(after(self.own, *gate), "c")
            return self.near

        def over_x(self, *gate):
            far = 1 - at_x
            own = self.product((at_c * xs + far) * part, part, gate, far * part)
            self.across = swap(own, "x")
            return own

        def over_z(self, *gate):
            across = after(self.across, *gate)
            total = self.product((at_c * xs + at_x) * part, part, gate, at_x * part, across)
            self.result = lax.psum_scatter(total, "z", scatter_dimension=self.dim, tiled=True)
            return total

        def over_z_first(self, *gate):
            total = self.product(at_c * xs * part, xs * part, gate, 0)
            self.both = lax.psum_scatter(total, "z", scatter_dimension=self.dim, tiled=True)
            return total

        def over_x_last(self, *gate):
            both = after(self.both, *gate)

            def take(x):
                return lax.dynamic_slice_in_dim(both, x * wide, wide, self.dim)

            self.result = take(at_x) + swap(take(1 - at_x), "x")
            return self.result

    features = inputs.astype(F32)
    unit1, scale1 = norm_parts(features)
    normed = (unit1 * norm1_gain + norm1_bias).astype(BF16)
    queries = (mm(normed, query_weight, ((1,), (0,))) + query_bias.reshape(-1)).astype(BF16)
    keys = mm(normed, key_weight, ((1,), (0,))).astype(BF16)
    values = (mm(normed, value_weight, ((1,), (0,))) + value_bias.reshape(-1)).astype(BF16)
    totals_log, attn_parts, mixed_blocks = [], [], []
    for block in range(block_count):
        mixed_block, log_total = attend(queries, keys, values, prefix_len, block, block_rows, head_dim)
        totals_log.append(log_total)
        mixed_blocks.append(mixed_block)
        for begin in range(0, block_rows, chunk):
            attn_parts.append(mm(mixed_block[begin : begin + chunk], out_weight, ((1,), (0,))))
    mixed = jnp.concatenate(mixed_blocks, 0)
    attn_others = [swap(piece, "mp") for piece in attn_parts]

    normed_pieces = pieces(normed)
    grad_pieces = [pieces(out_grad, True), pieces(out_grad)]
    early = [None, normed_pieces, *grad_pieces]
    resids, units2, scales2, normeds2 = [], [], [], []
    shares, pull_sums, kept = [], [], None
    for index in range(CHUNKS):
        rows = slice(index * chunk, (index + 1) * chunk)
        attn_other = attn_others[index]
        if index == 0:
            attn_other = after(attn_other, attn_parts[-1])
        else:
            attn_other = after(attn_other, pull_sums[-1], early[index % 4])
        resid = features[rows] + ((attn_parts[index] + attn_other) + out_bias)
        unit2, scale2 = norm_parts(resid)
        normed2 = (unit2 * norm2_gain + norm2_bias).astype(BF16)
        kept = hidden_step(
            normed2, out_grad, up_weight, up_bias.reshape(1, -1), down_weight, index, CHUNKS, kept
        )
        if index % 2:
            shares.append(kept[2])
        pull_sums.append(kept[3])
        resids.append(resid)
        units2.append(unit2)
        scales2.append(scale2)
        normeds2.append(normed2)
    acts, hidden_grads = kept[0], kept[1]
    up_bias_grad = sum(pull_sums)[0]
    share_others = [swap(after(shares[0], attn_others[-1]), "mp")]
    share_others.append(swap(shares[1], "mp"))

    grad_float = out_grad.astype(F32)
    down_bias_grad = jnp.sum(grad_float, 0)
    half = up_weight.shape[1] // 2
    normed2_pieces = pieces(jnp.concatenate(normeds2, 0))
    downs = [
        Sum(parts, acts, False, begin, half) for parts, begin in zip(grad_pieces, (0, half))
    ]
    ups = [Sum(normed2_pieces, hidden_grads, True, begin, half) for begin in (0, half)]

    resid_grads, attn_grads, mixed_grads = [], [], []
    norm2_gain_grad, norm2_bias_grad, out_bias_grad = 0.0, 0.0, 0.0

    def norm2_pull(pair, *gate):
        nonlocal norm2_gain_grad, norm2_bias_grad, out_bias_grad
        rows = slice(pair * 2 * chunk, (pair + 1) * 2 * chunk)
        unit2 = jnp.concatenate(units2[2 * pair : 2 * pair + 2], 0)
        scale2 = jnp.concatenate(scales2[2 * pair : 2 * pair + 2], 0)
        norm2_in = shares[pair] + after(share_others[pair], *gate)
        norm2_bias_grad = norm2_bias_grad + jnp.sum(norm2_in, 0)
        norm2_gain_grad = norm2_gain_grad + jnp.sum(norm2_in * unit2, 0)
        resid_grad = grad_float[rows] + norm_pull(norm2_in, unit2, scale2, norm2_gain)
        attn_grad = resid_grad.astype(BF16)
        out_bias_grad = out_bias_grad + jnp.sum(attn_grad.astype(F32), 0)
        mixed_grads.append(mm(attn_grad, out_weight, ((1,), (1,))).astype(BF16))
        resid_grads.append(resid_grad)
        attn_grads.append(attn_grad)
        return mixed_grads[-1]

    gate = downs[0].over_cores(kept[3])
    gate = downs[0].meet(gate)
    gate = downs[0].over_z_first(gate)
    gate = downs[1].over_cores(gate)
    gate = downs[1].meet(gate)
    gate = downs[1].over_x(gate)
    gate = ups[0].over_cores(gate)
    gate = ups[0].meet(gate)
    gate = ups[0].over_x(gate)
    gate = norm2_pull(0, gate)
    gate = downs[1].over_z(gate)
    branch = product_down(after(acts, gate), down_weight)
    gate = ups[1].over_cores(branch)
    gate = norm2_pull(1, gate)
    branch_other = swap(after(branch, share_others[-1]), "mp")
    gate = ups[0].over_z(gate)
    attn_grad = jnp.concatenate(attn_grads, 0)
    out_sum = Sum(pieces(attn_grad), mixed, False)
    gate = out_sum.over_cores(gate)
    gate = out_sum.meet(gate)
    gate = out_sum.over_x(gate)
    gate = ups[1].meet(gate)
    gate = ups[1].over_x(gate)
    mixed_grad = jnp.concatenate(mixed_grads, 0)
    query_grad, key_grad, value_grad, query_bias_grad, value_bias_grad = attend_pull(
        queries, keys, values, after(mixed_grad, gate), totals_log, prefix_len, head_dim
    )
    gate = query_bias_grad

    spans = [(0, 3 * length // 4), (3 * length // 4, length)]
    resid_grad = jnp.concatenate(resid_grads, 0)
    norm1_parts = []
    pulls = [after(query_grad, gate), key_grad, value_grad]
    for begin, end in spans:
        rows = end - begin
        norm1_parts.append(product_back(pulls, [query_weight, key_weight, value_weight], rows, begin // rows))
    norm1_others = [swap(piece, "mp") for piece in norm1_parts]

    query_sum, key_sum, value_sum = [
        Sum(normed_pieces, pull, True) for pull in (query_grad, key_grad, value_grad)
    ]
    sums = [query_sum, key_sum, value_sum]
    gate = out_sum.over_z(*norm1_parts)
    for item in sums:
        gate = item.over_cores(gate)
    gate = sums[-1].own
    for item in sums:
        gate = item.meet(gate)
    gate = query_sum.over_x(gate)
    gate = key_sum.over_x(gate)
    gate = ups[1].over_z(gate, branch_other)
    gate = value_sum.over_x(gate)
    outputs = (jnp.concatenate(resids, 0) + ((branch + after(branch_other, gate)) + down_bias)).astype(BF16)
    gate = outputs

    norm1_gain_grad, norm1_bias_grad = 0.0, 0.0
    in_grads = []

    def norm1_pull(index, gate):
        nonlocal norm1_gain_grad, norm1_bias_grad
        rows = slice(*spans[index])
        norm1_in = norm1_parts[index] + after(norm1_others[index], gate)
        norm1_bias_grad = norm1_bias_grad + jnp.sum(norm1_in, 0)
        norm1_gain_grad = norm1_gain_grad + jnp.sum(norm1_in * unit1[rows], 0)
        pulled = norm_pull(norm1_in, unit1[rows], scale1[rows], norm1_gain)
        in_grads.append((resid_grad[rows] + pulled).astype(BF16))
        return in_grads[-1]

    gate = query_sum.over_z(gate)
    gate = key_sum.over_z(gate)
    downs[0].over_x_last(gate)
    gate = norm1_pull(0, gate)
    gate = value_sum.over_z(gate)
    gate = norm1_pull(1, gate)
    in_grad = jnp.concatenate(in_grads, 0)

    def blocks(vector, lead):
        return jnp.transpose(vector.reshape(lead, dps, -1), (1, 0, 2)).reshape(dps, -1)

    small = jnp.concatenate(
        [
            blocks(norm1_gain_grad, 1),
            blocks(norm1_bias_grad, 1),
            blocks(query_bias_grad, heads_local),
            blocks(value_bias_grad, heads_local),
            blocks(out_bias_grad, 1),
            blocks(norm2_gain_grad, 1),
            blocks(norm2_bias_grad, 1),
            blocks(up_bias_grad, up_bias.shape[0]),
            blocks(down_bias_grad, 1),
        ],
        1,
    )
    small = small.reshape(zs, xs, cs, -1)

    def fold(field, axis, at, dim):
        def take(index):
            return lax.dynamic_index_in_dim(field, index, dim, keepdims=False)

        return take(at) + swap(take(1 - at), axis)

    small = fold(small, "c", at_c, 2)
    small = fold(small, "x", at_x, 1)
    at_z, span = lax.axis_index("z"), zs
    while span > 1:
        span //= 2
        halved = small.reshape(2, span, -1)
        side = (at_z // span) % 2
        pairs = [(i, i ^ span) for i in range(zs)]
        mine = lax.dynamic_index_in_dim(halved, side, 0, keepdims=False)
        other = lax.dynamic_index_in_dim(halved, 1 - side, 0, keepdims=False)
        small = mine + lax.ppermute(other, "z", pairs)
    small = small.reshape(-1)

    down_weight_grad = jnp.concatenate([item.result for item in downs], 0)
    up_weight_grad = jnp.concatenate([item.result for item in ups], 1)

    thin = head_dim // dps
    sizes = [wide, wide, heads_local * thin, heads_local * thin, wide, wide, wide]
    sizes += [up_bias.shape[0] * thin, wide]
    split, begin = [], 0
    for size in sizes:
        split.append(small[begin : begin + size])
        begin += size
    gain1, bias1, query_b, value_b, out_b, gain2, bias2, up_b, down_b = split
    return (
        outputs,
        in_grad,
        gain1,
        bias1,
        query_sum.result,
        query_b.reshape(heads_local, thin),
        key_sum.result,
        value_sum.result,
        value_b.reshape(heads_local, thin),
        out_sum.result,
        out_b,
        gain2,
        bias2,
        up_weight_grad,
        up_b.reshape(-1, thin),
        down_weight_grad,
        down_b,
    )


def solution(mesh):
    dps = mesh.shape["dp"]
    fine = Mesh(mesh.devices.reshape(dps // 4, 2, 2, mesh.shape["mp"]), ("z", "x", "c", "mp"))
    dp = ("z", "x", "c")
    in_specs = (
        P(dp, None),
        P(dp),
        P(),
        P(),
        P(None, "mp"),
        P("mp", None),
        P(None, "mp"),
        P(None, "mp"),
        P("mp", None),
        P("mp", None),
        P(),
        P(),
        P(),
        P(None, "mp"),
        P("mp", None),
        P("mp", None),
        P(),
        P(dp, None),
    )
    out_specs = (
        P(dp, None),
        P(dp, None),
        P(dp),
        P(dp),
        P(dp, "mp"),
        P("mp", dp),
        P(dp, "mp"),
        P(dp, "mp"),
        P("mp", dp),
        P("mp", dp),
        P(dp),
        P(dp),
        P(dp),
        P(dp, "mp"),
        P("mp", dp),
        P("mp", dp),
        P(dp),
    )
    return jax.shard_map(body, mesh=fine, in_specs=in_specs, out_specs=out_specs, check_vma=False)
```

```python
import math

import jax
import jax.numpy as jnp
from jax import lax
from jax.experimental import pallas as pl
from jax.experimental.pallas import tpu as pltpu
from jax.sharding import Mesh
from jax.sharding import PartitionSpec as P

F32 = jnp.float32
BF16 = jnp.bfloat16
CHUNKS = 4


def swap(value, axis):
    return lax.ppermute(value, axis, [(0, 1), (1, 0)])


def mm(left, right, contract):
    return lax.dot_general(left, right, (contract, ((), ())), preferred_element_type=F32)


def norm_parts(field):
    average = jnp.mean(field, -1, keepdims=True)
    centred = field - average
    variance = jnp.mean(centred * centred, -1, keepdims=True)
    scale = lax.rsqrt(variance + 1e-05)
    return centred * scale, scale


def norm_pull(grad, unit, scale, gain):
    scaled = grad * gain
    first = jnp.mean(scaled, -1, keepdims=True)
    second = jnp.mean(scaled * unit, -1, keepdims=True)
    return scale * (scaled - first - unit * second)


def after(value, *others):
    return lax.optimization_barrier((value,) + others)[0]


def blank(shape):
    return pl.pallas_call(
        lambda out_ref: None,
        out_specs=pl.BlockSpec(memory_space=pl.ANY),
        out_shape=jax.ShapeDtypeStruct(shape, F32),
    )()


def fitting(size, most):
    block = min(size, most)
    while size % block:
        block //= 2
    return block


def paired(left, right, left_at, right_at, shape, near=None, near_at=None, extra=None):
    length = left.shape[0]
    rows, cols = fitting(shape[0], 512), fitting(shape[1], 1024)
    near_at = near_at or (0, 0)
    starts = jnp.stack(
        [
            jnp.int32(left_at // rows),
            jnp.int32(right_at // cols),
            jnp.int32(near_at[0] // rows),
            jnp.int32(near_at[1] // cols),
        ]
    )

    def kernel(starts_ref, left_ref, right_ref, *rest):
        total = mm(left_ref[...], right_ref[...], ((0,), (0,)))
        for ref in rest[:-1]:
            total = total + ref[...]
        rest[-1][...] = total

    out_spec = pl.BlockSpec((rows, cols), lambda i, j, starts: (i, j))
    in_specs = [
        pl.BlockSpec((length, rows), lambda i, j, starts: (0, starts[0] + i)),
        pl.BlockSpec((length, cols), lambda i, j, starts: (0, starts[1] + j)),
    ]
    operands = [left, right]
    if near is not None:
        in_specs.append(pl.BlockSpec((rows, cols), lambda i, j, starts: (starts[2] + i, starts[3] + j)))
        operands.append(near)
    if extra is not None:
        in_specs.append(out_spec)
        operands.append(extra)
    return pl.pallas_call(
        kernel,
        grid_spec=pltpu.PrefetchScalarGridSpec(
            num_scalar_prefetch=1,
            grid=(shape[0] // rows, shape[1] // cols),
            in_specs=in_specs,
            out_specs=out_spec,
        ),
        out_shape=jax.ShapeDtypeStruct(shape, F32),
    )(starts, *operands)


def product_down(left, right):
    rows, inner = left.shape
    cols = right.shape[1]
    deep, wide = fitting(inner, 2048), fitting(cols, 512)

    def kernel(left_ref, right_ref, out_ref):
        share = mm(left_ref[...], right_ref[...], ((1,), (0,)))

        @pl.when(pl.program_id(1) == 0)
        def _():
            out_ref[...] = share

        @pl.when(pl.program_id(1) > 0)
        def _():
            out_ref[...] += share

    return pl.pallas_call(
        kernel,
        grid=(cols // wide, inner // deep),
        in_specs=[
            pl.BlockSpec((rows, deep), lambda j, k: (0, k)),
            pl.BlockSpec((deep, wide), lambda j, k: (k, j)),
        ],
        out_specs=pl.BlockSpec((rows, wide), lambda j, k: (0, j)),
        out_shape=jax.ShapeDtypeStruct((rows, cols), F32),
    )(left, right)


def product_back(pulls, weights, rows, index):
    span = pulls[0].shape[1]
    cols = weights[0].shape[0]
    wide = fitting(cols, 512)
    count = len(pulls)

    def kernel(*refs):
        total = mm(refs[0][...], refs[count][...], ((1,), (1,)))
        for at in range(1, count):
            total = total + mm(refs[at][...], refs[count + at][...], ((1,), (1,)))
        refs[-1][...] = total

    return pl.pallas_call(
        kernel,
        grid=(cols // wide,),
        in_specs=[pl.BlockSpec((rows, span), lambda j: (index, 0))] * count
        + [pl.BlockSpec((wide, span), lambda j: (j, 0))] * count,
        out_specs=pl.BlockSpec((rows, wide), lambda j: (0, j)),
        out_shape=jax.ShapeDtypeStruct((rows, cols), F32),
    )(*pulls, *weights)


def rows_of(count, begin, seen, boundary):
    rows = begin + lax.broadcasted_iota(jnp.int32, (count, seen), 0)
    cols = lax.broadcasted_iota(jnp.int32, (count, seen), 1)
    return (cols <= rows) | (cols < boundary)


def attend(queries, keys, values, boundary, block, block_rows, head_dim):
    length, span = queries.shape
    heads = span // head_dim
    tile = min(256, block_rows)
    scale = 1.0 / math.sqrt(head_dim)

    def kernel(boundary_ref, query_ref, key_ref, value_ref, mixed_ref, log_ref):
        for at in range(0, block_rows, tile):
            begin = block * block_rows + at
            seen = max(begin + tile, length // 2)
            scores = mm(query_ref[at : at + tile, :], key_ref[:seen, :], ((1,), (1,))) * scale
            scores = jnp.where(rows_of(tile, begin, seen, boundary_ref[0]), scores, -1e30)
            peak = jnp.max(scores, -1, keepdims=True)
            exps = jnp.exp(scores - peak)
            sums = jnp.sum(exps, -1, keepdims=True)
            log_ref[0, at : at + tile, :] = peak + jnp.log(sums)
            probs = (exps / sums).astype(BF16)
            mixed = mm(probs, value_ref[:seen, :], ((1,), (0,)))
            mixed_ref[at : at + tile, :] = mixed.astype(BF16)

    whole = pl.BlockSpec((length, head_dim), lambda head: (0, head))
    return pl.pallas_call(
        kernel,
        grid=(heads,),
        in_specs=[
            pl.BlockSpec(memory_space=pltpu.SMEM),
            pl.BlockSpec((block_rows, head_dim), lambda head: (block, head)),
            whole,
            whole,
        ],
        out_specs=[
            pl.BlockSpec((block_rows, head_dim), lambda head: (0, head)),
            pl.BlockSpec((1, block_rows, 1), lambda head: (head, 0, 0)),
        ],
        out_shape=[
            jax.ShapeDtypeStruct((block_rows, span), BF16),
            jax.ShapeDtypeStruct((heads, block_rows, 1), F32),
        ],
    )(boundary, queries, keys, values)


def attend_pull(queries, keys, values, mixed_grad, totals_log, boundary, head_dim):
    length, span = queries.shape
    heads = span // head_dim
    block_rows = totals_log[0].shape[1]
    tile = min(256, block_rows)
    scale = 1.0 / math.sqrt(head_dim)
    blocks = len(totals_log)

    def kernel(boundary_ref, query_ref, key_ref, value_ref, mixed_ref, *rest):
        log_refs, (dq_ref, dk_ref, dv_ref, qb_ref, vb_ref, dk_acc, dv_acc) = rest[:blocks], rest[blocks:]
        dk_acc[...] = jnp.zeros_like(dk_acc)
        dv_acc[...] = jnp.zeros_like(dv_acc)
        query_sum = jnp.zeros((1, head_dim), F32)
        for begin in range(0, length, tile):
            seen = max(begin + tile, length // 2)
            rows = slice(begin, begin + tile)
            query = query_ref[rows, :]
            mixed = mixed_ref[rows, :]
            inner = begin % block_rows
            log_total = log_refs[begin // block_rows][0, inner : inner + tile, :]
            scores = mm(query, key_ref[:seen, :], ((1,), (1,))) * scale
            scores = jnp.where(rows_of(tile, begin, seen, boundary_ref[0]), scores, -1e30)
            probs = jnp.exp(scores - log_total)
            prob_grad = mm(mixed, value_ref[:seen, :], ((1,), (1,)))
            row_dot = jnp.sum(probs * prob_grad, -1, keepdims=True)
            score_grad = (probs * (prob_grad - row_dot) * scale).astype(BF16)
            query_grad = mm(score_grad, key_ref[:seen, :], ((1,), (0,))).astype(BF16)
            dq_ref[rows, :] = query_grad
            query_sum = query_sum + jnp.sum(query_grad.astype(F32), 0, keepdims=True)
            dk_acc[:seen, :] += mm(score_grad, query, ((0,), (0,)))
            dv_acc[:seen, :] += mm(probs.astype(BF16), mixed, ((0,), (0,)))
        dk_ref[...] = dk_acc[...].astype(BF16)
        value_grad = dv_acc[...].astype(BF16)
        dv_ref[...] = value_grad
        qb_ref[0] = query_sum
        vb_ref[0] = jnp.sum(value_grad.astype(F32), 0, keepdims=True)

    whole = pl.BlockSpec((length, head_dim), lambda head: (0, head))
    line = pl.BlockSpec((1, 1, head_dim), lambda head: (head, 0, 0))
    return pl.pallas_call(
        kernel,
        grid=(heads,),
        in_specs=[pl.BlockSpec(memory_space=pltpu.SMEM)]
        + [whole] * 4
        + [pl.BlockSpec((1, block_rows, 1), lambda head: (head, 0, 0))] * blocks,
        out_specs=[whole] * 3 + [line] * 2,
        out_shape=[jax.ShapeDtypeStruct((length, span), BF16)] * 3
        + [jax.ShapeDtypeStruct((heads, 1, head_dim), F32)] * 2,
        scratch_shapes=[pltpu.VMEM((length, head_dim), F32)] * 2,
    )(boundary, queries, keys, values, mixed_grad, *totals_log)


def hidden_step(normed2, dy, up_weight, up_bias, down_weight, index, count, kept):
    chunk, width = normed2.shape
    local = up_weight.shape[1]
    block = min(512, local)
    pair = index % 2

    def kernel(normed_ref, dy_ref, up_ref, bias_ref, down_ref, *rest):
        act_ref, pull_ref, norm_ref, sum_ref = rest[-4:]
        hidden = mm(normed_ref[...], up_ref[...], ((1,), (0,))) + bias_ref[...]
        acts_grad = mm(dy_ref[...], down_ref[...], ((1,), (1,)))
        half = 0.5 * (1.0 + lax.erf(hidden * math.sqrt(0.5)))
        act_ref[...] = (hidden * half).astype(BF16)
        slope = half + hidden * (jnp.exp(-0.5 * hidden * hidden) * (1.0 / math.sqrt(2.0 * math.pi)))
        pull = (acts_grad * slope).astype(BF16)
        pull_ref[...] = pull
        sum_ref[...] = jnp.sum(pull.astype(F32), 0, keepdims=True)
        share = mm(pull, up_ref[...], ((1,), (1,)))

        @pl.when(pl.program_id(0) == 0)
        def _():
            norm_ref[...] = share

        @pl.when(pl.program_id(0) > 0)
        def _():
            norm_ref[...] += share

    same = pl.BlockSpec((chunk, width), lambda at: (0, 0))
    wide = pl.BlockSpec((chunk, block), lambda at: (index, at))
    line = pl.BlockSpec((1, block), lambda at: (0, at))
    held = [] if kept is None else [kept[0], kept[1]] + ([kept[2]] if pair else [])
    return pl.pallas_call(
        kernel,
        grid=(local // block,),
        in_specs=[
            same,
            pl.BlockSpec((chunk, width), lambda at: (index, 0)),
            pl.BlockSpec((width, block), lambda at: (0, at)),
            line,
            pl.BlockSpec((block, width), lambda at: (at, 0)),
        ]
        + [pl.BlockSpec(memory_space=pl.ANY)] * len(held),
        out_specs=[wide, wide, pl.BlockSpec((chunk, width), lambda at: (pair, 0)), line],
        out_shape=[
            jax.ShapeDtypeStruct((chunk * count, local), BF16),
            jax.ShapeDtypeStruct((chunk * count, local), BF16),
            jax.ShapeDtypeStruct((2 * chunk, width), F32),
            jax.ShapeDtypeStruct((1, local), F32),
        ],
        input_output_aliases={5 + at: at for at in range(len(held))},
    )(normed2, dy, up_weight, up_bias, down_weight, *held)


def body(
    inputs,
    prefix_len,
    norm1_gain,
    norm1_bias,
    query_weight,
    query_bias,
    key_weight,
    value_weight,
    value_bias,
    out_weight,
    out_bias,
    norm2_gain,
    norm2_bias,
    up_weight,
    up_bias,
    down_weight,
    down_bias,
    out_grad,
):
    length, width = inputs.shape
    heads_local, head_dim = query_bias.shape
    zs, xs, cs = lax.axis_size("z"), lax.axis_size("x"), lax.axis_size("c")
    dps = zs * xs * cs
    at_x, at_c = lax.axis_index("x"), lax.axis_index("c")
    wide = width // dps
    part = zs * wide
    block_rows = min(512, length)
    block_count = length // block_rows
    chunk = length // CHUNKS

    def pieces(field, by_z=False):
        if wide % 128:
            parts = field.reshape(length, zs, xs, cs, wide)
            return jnp.transpose(parts, (0, 3, 1, 2, 4) if by_z else (0, 3, 2, 1, 4)).reshape(field.shape)

        def source(at):
            c, rest = at // (xs * zs), at % (xs * zs)
            if by_z:
                return (0, rest * cs + c)
            return (0, ((rest % zs) * xs + rest // zs) * cs + c)

        def kernel(field_ref, out_ref):
            out_ref[...] = field_ref[...]

        return pl.pallas_call(
            kernel,
            grid=(dps,),
            in_specs=[pl.BlockSpec((length, wide), source)],
            out_specs=pl.BlockSpec((length, wide), lambda at: (0, at)),
            out_shape=jax.ShapeDtypeStruct(field.shape, field.dtype),
        )(field)

    once = jnp.minimum(prefix_len[0], 1)

    def swap_now(value, axis):
        def step(state):
            return (state[0] + 1, state[1], swap(after(state[1], state[0]), axis))

        start = (jnp.int32(0), value, blank(value.shape))
        return lax.while_loop(lambda state: state[0] < once, step, start)[2]

    class Sum:
        def __init__(self, parts, other, by_rows, begin=0, size=None):
            self.parts, self.other, self.by_rows = parts, other, by_rows
            self.dim = 0 if by_rows else 1
            self.begin = begin
            self.size = size or other.shape[1]

        def product(self, begin, size, gate, near_at=None, extra=None):
            other = after(self.other, *gate)
            near = None if near_at is None else self.near
            if self.by_rows:
                at = None if near_at is None else (near_at, 0)
                return paired(self.parts, other, begin, self.begin, (size, self.size), near, at, extra)
            at = None if near_at is None else (0, near_at)
            return paired(other, self.parts, self.begin, begin, (self.size, size), near, at, extra)

        def over_cores(self, *gate):
            own = self.product((1 - at_c) * xs * part, xs * part, gate)
            self.own = own
            return own

        def meet(self, *gate):
            self.near = swap_now(after(self.own, *gate), "c")
            return self.near

        def over_x(self, *gate):
            far = 1 - at_x
            own = self.product((at_c * xs + far) * part, part, gate, far * part)
            self.across = swap(own, "x")
            return own

        def over_z(self, *gate):
            across = after(self.across, *gate)
            total = self.product((at_c * xs + at_x) * part, part, gate, at_x * part, across)
            self.result = lax.psum_scatter(total, "z", scatter_dimension=self.dim, tiled=True)
            return total

        def over_z_first(self, *gate):
            total = self.product(at_c * xs * part, xs * part, gate, 0)
            self.both = lax.psum_scatter(total, "z", scatter_dimension=self.dim, tiled=True)
            return total

        def over_x_last(self, *gate):
            both = after(self.both, *gate)

            def take(x):
                return lax.dynamic_slice_in_dim(both, x * wide, wide, self.dim)

            self.result = take(at_x) + swap(take(1 - at_x), "x")
            return self.result

    features = inputs.astype(F32)
    unit1, scale1 = norm_parts(features)
    normed = (unit1 * norm1_gain + norm1_bias).astype(BF16)
    queries = (mm(normed, query_weight, ((1,), (0,))) + query_bias.reshape(-1)).astype(BF16)
    keys = mm(normed, key_weight, ((1,), (0,))).astype(BF16)
    values = (mm(normed, value_weight, ((1,), (0,))) + value_bias.reshape(-1)).astype(BF16)
    totals_log, attn_parts, mixed_blocks = [], [], []
    for block in range(block_count):
        mixed_block, log_total = attend(queries, keys, values, prefix_len, block, block_rows, head_dim)
        totals_log.append(log_total)
        mixed_blocks.append(mixed_block)
        for begin in range(0, block_rows, chunk):
            attn_parts.append(mm(mixed_block[begin : begin + chunk], out_weight, ((1,), (0,))))
    mixed = jnp.concatenate(mixed_blocks, 0)
    attn_others = [swap(piece, "mp") for piece in attn_parts]

    normed_pieces = pieces(normed)
    grad_pieces = [pieces(out_grad, True), pieces(out_grad)]
    early = [None, normed_pieces, *grad_pieces]
    resids, units2, scales2, normeds2 = [], [], [], []
    shares, pull_sums, kept = [], [], None
    for index in range(CHUNKS):
        rows = slice(index * chunk, (index + 1) * chunk)
        attn_other = attn_others[index]
        if index == 0:
            attn_other = after(attn_other, attn_parts[-1])
        else:
            attn_other = after(attn_other, pull_sums[-1], early[index % 4])
        resid = features[rows] + ((attn_parts[index] + attn_other) + out_bias)
        unit2, scale2 = norm_parts(resid)
        normed2 = (unit2 * norm2_gain + norm2_bias).astype(BF16)
        kept = hidden_step(
            normed2, out_grad, up_weight, up_bias.reshape(1, -1), down_weight, index, CHUNKS, kept
        )
        if index % 2:
            shares.append(kept[2])
        pull_sums.append(kept[3])
        resids.append(resid)
        units2.append(unit2)
        scales2.append(scale2)
        normeds2.append(normed2)
    acts, hidden_grads = kept[0], kept[1]
    up_bias_grad = sum(pull_sums)[0]
    share_others = [swap(after(shares[0], attn_others[-1]), "mp")]
    share_others.append(swap(shares[1], "mp"))

    grad_float = out_grad.astype(F32)
    down_bias_grad = jnp.sum(grad_float, 0)
    half = up_weight.shape[1] // 2
    normed2_pieces = pieces(jnp.concatenate(normeds2, 0))
    downs = [
        Sum(parts, acts, False, begin, half) for parts, begin in zip(grad_pieces, (0, half))
    ]
    ups = [Sum(normed2_pieces, hidden_grads, True, begin, half) for begin in (0, half)]

    resid_grads, attn_grads, mixed_grads = [], [], []
    norm2_gain_grad, norm2_bias_grad, out_bias_grad = 0.0, 0.0, 0.0

    def norm2_pull(pair, *gate):
        nonlocal norm2_gain_grad, norm2_bias_grad, out_bias_grad
        rows = slice(pair * 2 * chunk, (pair + 1) * 2 * chunk)
        unit2 = jnp.concatenate(units2[2 * pair : 2 * pair + 2], 0)
        scale2 = jnp.concatenate(scales2[2 * pair : 2 * pair + 2], 0)
        norm2_in = shares[pair] + after(share_others[pair], *gate)
        norm2_bias_grad = norm2_bias_grad + jnp.sum(norm2_in, 0)
        norm2_gain_grad = norm2_gain_grad + jnp.sum(norm2_in * unit2, 0)
        resid_grad = grad_float[rows] + norm_pull(norm2_in, unit2, scale2, norm2_gain)
        attn_grad = resid_grad.astype(BF16)
        out_bias_grad = out_bias_grad + jnp.sum(attn_grad.astype(F32), 0)
        mixed_grads.append(mm(attn_grad, out_weight, ((1,), (1,))).astype(BF16))
        resid_grads.append(resid_grad)
        attn_grads.append(attn_grad)
        return mixed_grads[-1]

    gate = downs[0].over_cores(kept[3])
    gate = downs[0].meet(gate)
    gate = downs[0].over_z_first(gate)
    gate = downs[1].over_cores(gate)
    gate = downs[1].meet(gate)
    gate = downs[1].over_x(gate)
    gate = ups[0].over_cores(gate)
    gate = ups[0].meet(gate)
    gate = ups[0].over_x(gate)
    gate = norm2_pull(0, gate)
    gate = downs[1].over_z(gate)
    branch = product_down(after(acts, gate), down_weight)
    gate = ups[1].over_cores(branch)
    gate = norm2_pull(1, gate)
    branch_other = swap(after(branch, share_others[-1]), "mp")
    gate = ups[1].meet(gate)
    gate = ups[1].over_x(gate)
    gate = ups[0].over_z(gate)
    mixed_grad = jnp.concatenate(mixed_grads, 0)
    attn_grad = jnp.concatenate(attn_grads, 0)
    query_grad, key_grad, value_grad, query_bias_grad, value_bias_grad = attend_pull(
        queries, keys, values, after(mixed_grad, gate), totals_log, prefix_len, head_dim
    )
    gate = query_bias_grad

    spans = [(0, 3 * length // 4), (3 * length // 4, length)]
    resid_grad = jnp.concatenate(resid_grads, 0)
    norm1_parts = []
    pulls = [after(query_grad, gate), key_grad, value_grad]
    for begin, end in spans:
        rows = end - begin
        norm1_parts.append(product_back(pulls, [query_weight, key_weight, value_weight], rows, begin // rows))
    norm1_others = [swap(piece, "mp") for piece in norm1_parts]

    out_sum = Sum(pieces(attn_grad), mixed, False)
    query_sum, key_sum, value_sum = [
        Sum(normed_pieces, pull, True) for pull in (query_grad, key_grad, value_grad)
    ]
    sums = [out_sum, query_sum, key_sum, value_sum]
    for item in sums:
        gate = item.over_cores(*norm1_parts)
    gate = sums[-1].own
    for item in sums:
        gate = item.meet(gate)
    gate = out_sum.over_x(gate)
    outputs = (jnp.concatenate(resids, 0) + ((branch + after(branch_other, gate)) + down_bias)).astype(BF16)
    gate = ups[1].over_z(outputs)
    gate = query_sum.over_x(gate)
    gate = out_sum.over_z(gate)
    gate = key_sum.over_x(gate)

    norm1_gain_grad, norm1_bias_grad = 0.0, 0.0
    in_grads = []

    def norm1_pull(index, gate):
        nonlocal norm1_gain_grad, norm1_bias_grad
        rows = slice(*spans[index])
        norm1_in = norm1_parts[index] + after(norm1_others[index], gate)
        norm1_bias_grad = norm1_bias_grad + jnp.sum(norm1_in, 0)
        norm1_gain_grad = norm1_gain_grad + jnp.sum(norm1_in * unit1[rows], 0)
        pulled = norm_pull(norm1_in, unit1[rows], scale1[rows], norm1_gain)
        in_grads.append((resid_grad[rows] + pulled).astype(BF16))
        return in_grads[-1]

    gate = query_sum.over_z(gate)
    gate = value_sum.over_x(gate)
    downs[0].over_x_last(gate)
    gate = norm1_pull(0, gate)
    gate = key_sum.over_z(gate)
    gate = norm1_pull(1, gate)
    gate = value_sum.over_z(gate)
    in_grad = jnp.concatenate(in_grads, 0)

    def blocks(vector, lead):
        return jnp.transpose(vector.reshape(lead, dps, -1), (1, 0, 2)).reshape(dps, -1)

    small = jnp.concatenate(
        [
            blocks(norm1_gain_grad, 1),
            blocks(norm1_bias_grad, 1),
            blocks(query_bias_grad, heads_local),
            blocks(value_bias_grad, heads_local),
            blocks(out_bias_grad, 1),
            blocks(norm2_gain_grad, 1),
            blocks(norm2_bias_grad, 1),
            blocks(up_bias_grad, up_bias.shape[0]),
            blocks(down_bias_grad, 1),
        ],
        1,
    )
    small = small.reshape(zs, xs, cs, -1)

    def fold(field, axis, at, dim):
        def take(index):
            return lax.dynamic_index_in_dim(field, index, dim, keepdims=False)

        return take(at) + swap(take(1 - at), axis)

    small = fold(small, "c", at_c, 2)
    small = fold(small, "x", at_x, 1)
    at_z, span = lax.axis_index("z"), zs
    while span > 1:
        span //= 2
        halved = small.reshape(2, span, -1)
        side = (at_z // span) % 2
        pairs = [(i, i ^ span) for i in range(zs)]
        mine = lax.dynamic_index_in_dim(halved, side, 0, keepdims=False)
        other = lax.dynamic_index_in_dim(halved, 1 - side, 0, keepdims=False)
        small = mine + lax.ppermute(other, "z", pairs)
    small = small.reshape(-1)

    down_weight_grad = jnp.concatenate([item.result for item in downs], 0)
    up_weight_grad = jnp.concatenate([item.result for item in ups], 1)

    thin = head_dim // dps
    sizes = [wide, wide, heads_local * thin, heads_local * thin, wide, wide, wide]
    sizes += [up_bias.shape[0] * thin, wide]
    split, begin = [], 0
    for size in sizes:
        split.append(small[begin : begin + size])
        begin += size
    gain1, bias1, query_b, value_b, out_b, gain2, bias2, up_b, down_b = split
    return (
        outputs,
        in_grad,
        gain1,
        bias1,
        query_sum.result,
        query_b.reshape(heads_local, thin),
        key_sum.result,
        value_sum.result,
        value_b.reshape(heads_local, thin),
        out_sum.result,
        out_b,
        gain2,
        bias2,
        up_weight_grad,
        up_b.reshape(-1, thin),
        down_weight_grad,
        down_b,
    )


def solution(mesh):
    dps = mesh.shape["dp"]
    fine = Mesh(mesh.devices.reshape(dps // 4, 2, 2, mesh.shape["mp"]), ("z", "x", "c", "mp"))
    dp = ("z", "x", "c")
    in_specs = (
        P(dp, None),
        P(dp),
        P(),
        P(),
        P(None, "mp"),
        P("mp", None),
        P(None, "mp"),
        P(None, "mp"),
        P("mp", None),
        P("mp", None),
        P(),
        P(),
        P(),
        P(None, "mp"),
        P("mp", None),
        P("mp", None),
        P(),
        P(dp, None),
    )
    out_specs = (
        P(dp, None),
        P(dp, None),
        P(dp),
        P(dp),
        P(dp, "mp"),
        P("mp", dp),
        P(dp, "mp"),
        P(dp, "mp"),
        P("mp", dp),
        P("mp", dp),
        P(dp),
        P(dp),
        P(dp),
        P(dp, "mp"),
        P("mp", dp),
        P("mp", dp),
        P(dp),
    )
    return jax.shard_map(body, mesh=fine, in_specs=in_specs, out_specs=out_specs, check_vma=False)
```

```python
import math

import jax
import jax.numpy as jnp
from jax import lax
from jax.experimental import pallas as pl
from jax.experimental.pallas import tpu as pltpu
from jax.sharding import Mesh
from jax.sharding import PartitionSpec as P

F32 = jnp.float32
BF16 = jnp.bfloat16
CHUNKS = 4


def swap(value, axis):
    return lax.ppermute(value, axis, [(0, 1), (1, 0)])


def mm(left, right, contract):
    return lax.dot_general(left, right, (contract, ((), ())), preferred_element_type=F32)


def norm_parts(field):
    average = jnp.mean(field, -1, keepdims=True)
    centred = field - average
    variance = jnp.mean(centred * centred, -1, keepdims=True)
    scale = lax.rsqrt(variance + 1e-05)
    return centred * scale, scale


def norm_pull(grad, unit, scale, gain):
    scaled = grad * gain
    first = jnp.mean(scaled, -1, keepdims=True)
    second = jnp.mean(scaled * unit, -1, keepdims=True)
    return scale * (scaled - first - unit * second)


def after(value, *others):
    return lax.optimization_barrier((value,) + others)[0]


def blank(shape):
    return pl.pallas_call(
        lambda out_ref: None,
        out_specs=pl.BlockSpec(memory_space=pl.ANY),
        out_shape=jax.ShapeDtypeStruct(shape, F32),
    )()


def fitting(size, most):
    block = min(size, most)
    while size % block:
        block //= 2
    return block


def paired(left, right, left_at, right_at, shape, near=None, near_at=None, extra=None):
    length = left.shape[0]
    rows, cols = fitting(shape[0], 512), fitting(shape[1], 1024)
    near_at = near_at or (0, 0)
    starts = jnp.stack(
        [
            jnp.int32(left_at // rows),
            jnp.int32(right_at // cols),
            jnp.int32(near_at[0] // rows),
            jnp.int32(near_at[1] // cols),
        ]
    )

    def kernel(starts_ref, left_ref, right_ref, *rest):
        total = mm(left_ref[...], right_ref[...], ((0,), (0,)))
        for ref in rest[:-1]:
            total = total + ref[...]
        rest[-1][...] = total

    out_spec = pl.BlockSpec((rows, cols), lambda i, j, starts: (i, j))
    in_specs = [
        pl.BlockSpec((length, rows), lambda i, j, starts: (0, starts[0] + i)),
        pl.BlockSpec((length, cols), lambda i, j, starts: (0, starts[1] + j)),
    ]
    operands = [left, right]
    if near is not None:
        in_specs.append(pl.BlockSpec((rows, cols), lambda i, j, starts: (starts[2] + i, starts[3] + j)))
        operands.append(near)
    if extra is not None:
        in_specs.append(out_spec)
        operands.append(extra)
    return pl.pallas_call(
        kernel,
        grid_spec=pltpu.PrefetchScalarGridSpec(
            num_scalar_prefetch=1,
            grid=(shape[0] // rows, shape[1] // cols),
            in_specs=in_specs,
            out_specs=out_spec,
        ),
        out_shape=jax.ShapeDtypeStruct(shape, F32),
    )(starts, *operands)


def product_down(left, right):
    rows, inner = left.shape
    cols = right.shape[1]
    deep, wide = fitting(inner, 2048), fitting(cols, 512)

    def kernel(left_ref, right_ref, out_ref):
        share = mm(left_ref[...], right_ref[...], ((1,), (0,)))

        @pl.when(pl.program_id(1) == 0)
        def _():
            out_ref[...] = share

        @pl.when(pl.program_id(1) > 0)
        def _():
            out_ref[...] += share

    return pl.pallas_call(
        kernel,
        grid=(cols // wide, inner // deep),
        in_specs=[
            pl.BlockSpec((rows, deep), lambda j, k: (0, k)),
            pl.BlockSpec((deep, wide), lambda j, k: (k, j)),
        ],
        out_specs=pl.BlockSpec((rows, wide), lambda j, k: (0, j)),
        out_shape=jax.ShapeDtypeStruct((rows, cols), F32),
    )(left, right)


def product_back(pulls, weights, rows, index):
    span = pulls[0].shape[1]
    cols = weights[0].shape[0]
    wide = fitting(cols, 512)
    count = len(pulls)

    def kernel(*refs):
        total = mm(refs[0][...], refs[count][...], ((1,), (1,)))
        for at in range(1, count):
            total = total + mm(refs[at][...], refs[count + at][...], ((1,), (1,)))
        refs[-1][...] = total

    return pl.pallas_call(
        kernel,
        grid=(cols // wide,),
        in_specs=[pl.BlockSpec((rows, span), lambda j: (index, 0))] * count
        + [pl.BlockSpec((wide, span), lambda j: (j, 0))] * count,
        out_specs=pl.BlockSpec((rows, wide), lambda j: (0, j)),
        out_shape=jax.ShapeDtypeStruct((rows, cols), F32),
    )(*pulls, *weights)


def rows_of(count, begin, seen, boundary):
    rows = begin + lax.broadcasted_iota(jnp.int32, (count, seen), 0)
    cols = lax.broadcasted_iota(jnp.int32, (count, seen), 1)
    return (cols <= rows) | (cols < boundary)


def attend(queries, keys, values, boundary, block, block_rows, head_dim):
    length, span = queries.shape
    heads = span // head_dim
    tile = min(256, block_rows)
    scale = 1.0 / math.sqrt(head_dim)

    def kernel(boundary_ref, query_ref, key_ref, value_ref, mixed_ref, log_ref):
        for at in range(0, block_rows, tile):
            begin = block * block_rows + at
            seen = max(begin + tile, length // 2)
            scores = mm(query_ref[at : at + tile, :], key_ref[:seen, :], ((1,), (1,))) * scale
            scores = jnp.where(rows_of(tile, begin, seen, boundary_ref[0]), scores, -1e30)
            peak = jnp.max(scores, -1, keepdims=True)
            exps = jnp.exp(scores - peak)
            sums = jnp.sum(exps, -1, keepdims=True)
            log_ref[0, at : at + tile, :] = peak + jnp.log(sums)
            probs = (exps / sums).astype(BF16)
            mixed = mm(probs, value_ref[:seen, :], ((1,), (0,)))
            mixed_ref[at : at + tile, :] = mixed.astype(BF16)

    whole = pl.BlockSpec((length, head_dim), lambda head: (0, head))
    return pl.pallas_call(
        kernel,
        grid=(heads,),
        in_specs=[
            pl.BlockSpec(memory_space=pltpu.SMEM),
            pl.BlockSpec((block_rows, head_dim), lambda head: (block, head)),
            whole,
            whole,
        ],
        out_specs=[
            pl.BlockSpec((block_rows, head_dim), lambda head: (0, head)),
            pl.BlockSpec((1, block_rows, 1), lambda head: (head, 0, 0)),
        ],
        out_shape=[
            jax.ShapeDtypeStruct((block_rows, span), BF16),
            jax.ShapeDtypeStruct((heads, block_rows, 1), F32),
        ],
    )(boundary, queries, keys, values)


def attend_pull(queries, keys, values, mixed_grad, totals_log, boundary, head_dim):
    length, span = queries.shape
    heads = span // head_dim
    block_rows = totals_log[0].shape[1]
    tile = min(256, block_rows)
    scale = 1.0 / math.sqrt(head_dim)
    blocks = len(totals_log)

    def kernel(boundary_ref, query_ref, key_ref, value_ref, mixed_ref, *rest):
        log_refs, (dq_ref, dk_ref, dv_ref, qb_ref, vb_ref, dk_acc, dv_acc) = rest[:blocks], rest[blocks:]
        dk_acc[...] = jnp.zeros_like(dk_acc)
        dv_acc[...] = jnp.zeros_like(dv_acc)
        query_sum = jnp.zeros((1, head_dim), F32)
        for begin in range(0, length, tile):
            seen = max(begin + tile, length // 2)
            rows = slice(begin, begin + tile)
            query = query_ref[rows, :]
            mixed = mixed_ref[rows, :]
            inner = begin % block_rows
            log_total = log_refs[begin // block_rows][0, inner : inner + tile, :]
            scores = mm(query, key_ref[:seen, :], ((1,), (1,))) * scale
            scores = jnp.where(rows_of(tile, begin, seen, boundary_ref[0]), scores, -1e30)
            probs = jnp.exp(scores - log_total)
            prob_grad = mm(mixed, value_ref[:seen, :], ((1,), (1,)))
            row_dot = jnp.sum(probs * prob_grad, -1, keepdims=True)
            score_grad = (probs * (prob_grad - row_dot) * scale).astype(BF16)
            query_grad = mm(score_grad, key_ref[:seen, :], ((1,), (0,))).astype(BF16)
            dq_ref[rows, :] = query_grad
            query_sum = query_sum + jnp.sum(query_grad.astype(F32), 0, keepdims=True)
            dk_acc[:seen, :] += mm(score_grad, query, ((0,), (0,)))
            dv_acc[:seen, :] += mm(probs.astype(BF16), mixed, ((0,), (0,)))
        dk_ref[...] = dk_acc[...].astype(BF16)
        value_grad = dv_acc[...].astype(BF16)
        dv_ref[...] = value_grad
        qb_ref[0] = query_sum
        vb_ref[0] = jnp.sum(value_grad.astype(F32), 0, keepdims=True)

    whole = pl.BlockSpec((length, head_dim), lambda head: (0, head))
    line = pl.BlockSpec((1, 1, head_dim), lambda head: (head, 0, 0))
    return pl.pallas_call(
        kernel,
        grid=(heads,),
        in_specs=[pl.BlockSpec(memory_space=pltpu.SMEM)]
        + [whole] * 4
        + [pl.BlockSpec((1, block_rows, 1), lambda head: (head, 0, 0))] * blocks,
        out_specs=[whole] * 3 + [line] * 2,
        out_shape=[jax.ShapeDtypeStruct((length, span), BF16)] * 3
        + [jax.ShapeDtypeStruct((heads, 1, head_dim), F32)] * 2,
        scratch_shapes=[pltpu.VMEM((length, head_dim), F32)] * 2,
    )(boundary, queries, keys, values, mixed_grad, *totals_log)


def hidden_step(normed2, dy, up_weight, up_bias, down_weight, index, count, kept):
    chunk, width = normed2.shape
    local = up_weight.shape[1]
    block = min(512, local)
    pair = index % 2

    def kernel(normed_ref, dy_ref, up_ref, bias_ref, down_ref, *rest):
        act_ref, pull_ref, norm_ref, sum_ref = rest[-4:]
        hidden = mm(normed_ref[...], up_ref[...], ((1,), (0,))) + bias_ref[...]
        acts_grad = mm(dy_ref[...], down_ref[...], ((1,), (1,)))
        half = 0.5 * (1.0 + lax.erf(hidden * math.sqrt(0.5)))
        act_ref[...] = (hidden * half).astype(BF16)
        slope = half + hidden * (jnp.exp(-0.5 * hidden * hidden) * (1.0 / math.sqrt(2.0 * math.pi)))
        pull = (acts_grad * slope).astype(BF16)
        pull_ref[...] = pull
        sum_ref[...] = jnp.sum(pull.astype(F32), 0, keepdims=True)
        share = mm(pull, up_ref[...], ((1,), (1,)))

        @pl.when(pl.program_id(0) == 0)
        def _():
            norm_ref[...] = share

        @pl.when(pl.program_id(0) > 0)
        def _():
            norm_ref[...] += share

    same = pl.BlockSpec((chunk, width), lambda at: (0, 0))
    wide = pl.BlockSpec((chunk, block), lambda at: (index, at))
    line = pl.BlockSpec((1, block), lambda at: (0, at))
    held = [] if kept is None else [kept[0], kept[1]] + ([kept[2]] if pair else [])
    return pl.pallas_call(
        kernel,
        grid=(local // block,),
        in_specs=[
            same,
            pl.BlockSpec((chunk, width), lambda at: (index, 0)),
            pl.BlockSpec((width, block), lambda at: (0, at)),
            line,
            pl.BlockSpec((block, width), lambda at: (at, 0)),
        ]
        + [pl.BlockSpec(memory_space=pl.ANY)] * len(held),
        out_specs=[wide, wide, pl.BlockSpec((chunk, width), lambda at: (pair, 0)), line],
        out_shape=[
            jax.ShapeDtypeStruct((chunk * count, local), BF16),
            jax.ShapeDtypeStruct((chunk * count, local), BF16),
            jax.ShapeDtypeStruct((2 * chunk, width), F32),
            jax.ShapeDtypeStruct((1, local), F32),
        ],
        input_output_aliases={5 + at: at for at in range(len(held))},
    )(normed2, dy, up_weight, up_bias, down_weight, *held)


def body(
    inputs,
    prefix_len,
    norm1_gain,
    norm1_bias,
    query_weight,
    query_bias,
    key_weight,
    value_weight,
    value_bias,
    out_weight,
    out_bias,
    norm2_gain,
    norm2_bias,
    up_weight,
    up_bias,
    down_weight,
    down_bias,
    out_grad,
):
    length, width = inputs.shape
    heads_local, head_dim = query_bias.shape
    zs, xs, cs = lax.axis_size("z"), lax.axis_size("x"), lax.axis_size("c")
    dps = zs * xs * cs
    at_x, at_c = lax.axis_index("x"), lax.axis_index("c")
    wide = width // dps
    part = zs * wide
    block_rows = min(512, length)
    block_count = length // block_rows
    chunk = length // CHUNKS

    def pieces(field, by_z=False):
        if wide % 128:
            parts = field.reshape(length, zs, xs, cs, wide)
            return jnp.transpose(parts, (0, 3, 1, 2, 4) if by_z else (0, 3, 2, 1, 4)).reshape(field.shape)

        def source(at):
            c, rest = at // (xs * zs), at % (xs * zs)
            if by_z:
                return (0, rest * cs + c)
            return (0, ((rest % zs) * xs + rest // zs) * cs + c)

        def kernel(field_ref, out_ref):
            out_ref[...] = field_ref[...]

        return pl.pallas_call(
            kernel,
            grid=(dps,),
            in_specs=[pl.BlockSpec((length, wide), source)],
            out_specs=pl.BlockSpec((length, wide), lambda at: (0, at)),
            out_shape=jax.ShapeDtypeStruct(field.shape, field.dtype),
        )(field)

    once = jnp.minimum(prefix_len[0], 1)

    def swap_now(value, axis):
        def step(state):
            return (state[0] + 1, state[1], swap(after(state[1], state[0]), axis))

        start = (jnp.int32(0), value, blank(value.shape))
        return lax.while_loop(lambda state: state[0] < once, step, start)[2]

    class Sum:
        def __init__(self, parts, other, by_rows, begin=0, size=None):
            self.parts, self.other, self.by_rows = parts, other, by_rows
            self.dim = 0 if by_rows else 1
            self.begin = begin
            self.size = size or other.shape[1]

        def product(self, begin, size, gate, near_at=None, extra=None):
            other = after(self.other, *gate)
            near = None if near_at is None else self.near
            if self.by_rows:
                at = None if near_at is None else (near_at, 0)
                return paired(self.parts, other, begin, self.begin, (size, self.size), near, at, extra)
            at = None if near_at is None else (0, near_at)
            return paired(other, self.parts, self.begin, begin, (self.size, size), near, at, extra)

        def over_cores(self, *gate):
            own = self.product((1 - at_c) * xs * part, xs * part, gate)
            self.own = own
            return own

        def meet(self, *gate):
            self.near = swap_now(after(self.own, *gate), "c")
            return self.near

        def over_x(self, *gate):
            far = 1 - at_x
            own = self.product((at_c * xs + far) * part, part, gate, far * part)
            self.across = swap(own, "x")
            return own

        def over_z(self, *gate):
            across = after(self.across, *gate)
            total = self.product((at_c * xs + at_x) * part, part, gate, at_x * part, across)
            self.result = lax.psum_scatter(total, "z", scatter_dimension=self.dim, tiled=True)
            return total

        def over_z_first(self, *gate):
            total = self.product(at_c * xs * part, xs * part, gate, 0)
            self.both = lax.psum_scatter(total, "z", scatter_dimension=self.dim, tiled=True)
            return total

        def over_x_last(self, *gate):
            both = after(self.both, *gate)

            def take(x):
                return lax.dynamic_slice_in_dim(both, x * wide, wide, self.dim)

            self.result = take(at_x) + swap(take(1 - at_x), "x")
            return self.result

    features = inputs.astype(F32)
    unit1, scale1 = norm_parts(features)
    normed = (unit1 * norm1_gain + norm1_bias).astype(BF16)
    queries = (mm(normed, query_weight, ((1,), (0,))) + query_bias.reshape(-1)).astype(BF16)
    keys = mm(normed, key_weight, ((1,), (0,))).astype(BF16)
    values = (mm(normed, value_weight, ((1,), (0,))) + value_bias.reshape(-1)).astype(BF16)
    totals_log, attn_parts, mixed_blocks = [], [], []
    for block in range(block_count):
        mixed_block, log_total = attend(queries, keys, values, prefix_len, block, block_rows, head_dim)
        totals_log.append(log_total)
        mixed_blocks.append(mixed_block)
        for begin in range(0, block_rows, chunk):
            attn_parts.append(mm(mixed_block[begin : begin + chunk], out_weight, ((1,), (0,))))
    mixed = jnp.concatenate(mixed_blocks, 0)
    attn_others = [swap(piece, "mp") for piece in attn_parts]

    normed_pieces = pieces(normed)
    grad_pieces = [pieces(out_grad, True), pieces(out_grad)]
    early = [None, normed_pieces, *grad_pieces]
    resids, units2, scales2, normeds2 = [], [], [], []
    shares, pull_sums, kept = [], [], None
    for index in range(CHUNKS):
        rows = slice(index * chunk, (index + 1) * chunk)
        attn_other = attn_others[index]
        if index == 0:
            attn_other = after(attn_other, attn_parts[-1])
        else:
            attn_other = after(attn_other, pull_sums[-1], early[index % 4])
        resid = features[rows] + ((attn_parts[index] + attn_other) + out_bias)
        unit2, scale2 = norm_parts(resid)
        normed2 = (unit2 * norm2_gain + norm2_bias).astype(BF16)
        kept = hidden_step(
            normed2, out_grad, up_weight, up_bias.reshape(1, -1), down_weight, index, CHUNKS, kept
        )
        if index % 2:
            shares.append(kept[2])
        pull_sums.append(kept[3])
        resids.append(resid)
        units2.append(unit2)
        scales2.append(scale2)
        normeds2.append(normed2)
    acts, hidden_grads = kept[0], kept[1]
    up_bias_grad = sum(pull_sums)[0]
    share_others = [swap(after(shares[0], attn_others[-1]), "mp")]
    share_others.append(swap(shares[1], "mp"))

    grad_float = out_grad.astype(F32)
    down_bias_grad = jnp.sum(grad_float, 0)
    half = up_weight.shape[1] // 2
    normed2_pieces = pieces(jnp.concatenate(normeds2, 0))
    downs = [
        Sum(parts, acts, False, begin, half) for parts, begin in zip(grad_pieces, (0, half))
    ]
    ups = [Sum(normed2_pieces, hidden_grads, True, begin, half) for begin in (0, half)]

    resid_grads, attn_grads, mixed_grads = [], [], []
    norm2_gain_grad, norm2_bias_grad, out_bias_grad = 0.0, 0.0, 0.0

    def norm2_pull(pair, *gate):
        nonlocal norm2_gain_grad, norm2_bias_grad, out_bias_grad
        rows = slice(pair * 2 * chunk, (pair + 1) * 2 * chunk)
        unit2 = jnp.concatenate(units2[2 * pair : 2 * pair + 2], 0)
        scale2 = jnp.concatenate(scales2[2 * pair : 2 * pair + 2], 0)
        norm2_in = shares[pair] + after(share_others[pair], *gate)
        norm2_bias_grad = norm2_bias_grad + jnp.sum(norm2_in, 0)
        norm2_gain_grad = norm2_gain_grad + jnp.sum(norm2_in * unit2, 0)
        resid_grad = grad_float[rows] + norm_pull(norm2_in, unit2, scale2, norm2_gain)
        attn_grad = resid_grad.astype(BF16)
        out_bias_grad = out_bias_grad + jnp.sum(attn_grad.astype(F32), 0)
        mixed_grads.append(mm(attn_grad, out_weight, ((1,), (1,))).astype(BF16))
        resid_grads.append(resid_grad)
        attn_grads.append(attn_grad)
        return mixed_grads[-1]

    gate = downs[0].over_cores(kept[3])
    gate = downs[0].meet(gate)
    gate = downs[0].over_z_first(gate)
    gate = downs[1].over_cores(gate)
    gate = downs[1].meet(gate)
    gate = downs[1].over_x(gate)
    gate = ups[0].over_cores(gate)
    gate = ups[0].meet(gate)
    gate = ups[0].over_x(gate)
    gate = norm2_pull(0, gate)
    gate = downs[1].over_z(gate)
    branch = product_down(after(acts, gate), down_weight)
    gate = ups[1].over_cores(branch)
    gate = norm2_pull(1, gate)
    branch_other = swap(after(branch, share_others[-1]), "mp")
    gate = ups[1].meet(gate)
    gate = ups[1].over_x(gate)
    gate = ups[0].over_z(gate)
    mixed_grad = jnp.concatenate(mixed_grads, 0)
    attn_grad = jnp.concatenate(attn_grads, 0)
    query_grad, key_grad, value_grad, query_bias_grad, value_bias_grad = attend_pull(
        queries, keys, values, after(mixed_grad, gate), totals_log, prefix_len, head_dim
    )
    gate = query_bias_grad

    spans = [(0, 3 * length // 4), (3 * length // 4, length)]
    resid_grad = jnp.concatenate(resid_grads, 0)
    norm1_parts = []
    pulls = [after(query_grad, gate), key_grad, value_grad]
    for begin, end in spans:
        rows = end - begin
        norm1_parts.append(product_back(pulls, [query_weight, key_weight, value_weight], rows, begin // rows))
    norm1_others = [swap(piece, "mp") for piece in norm1_parts]

    out_sum = Sum(pieces(attn_grad), mixed, False)
    query_sum, key_sum, value_sum = [
        Sum(normed_pieces, pull, True) for pull in (query_grad, key_grad, value_grad)
    ]
    sums = [out_sum, query_sum, key_sum, value_sum]
    for item in sums:
        gate = item.over_cores(*norm1_parts)
    gate = sums[-1].own
    for item in sums:
        gate = item.meet(gate)
    gate = out_sum.over_x(gate)

    def finish(begin, end, gate):
        rows = slice(begin * chunk, end * chunk)
        other = after(branch_other, gate)
        return (jnp.concatenate(resids[begin:end], 0) + ((branch[rows] + other[rows]) + down_bias)).astype(BF16)

    outputs = [finish(0, 1, gate)]
    gate = ups[1].over_z(outputs[0])
    gate = query_sum.over_x(gate)
    outputs.append(finish(1, CHUNKS, gate))
    outputs = jnp.concatenate(outputs, 0)
    gate = out_sum.over_z(gate)
    gate = key_sum.over_x(gate)

    norm1_gain_grad, norm1_bias_grad = 0.0, 0.0
    in_grads = []

    def norm1_pull(index, gate):
        nonlocal norm1_gain_grad, norm1_bias_grad
        rows = slice(*spans[index])
        norm1_in = norm1_parts[index] + after(norm1_others[index], gate)
        norm1_bias_grad = norm1_bias_grad + jnp.sum(norm1_in, 0)
        norm1_gain_grad = norm1_gain_grad + jnp.sum(norm1_in * unit1[rows], 0)
        pulled = norm_pull(norm1_in, unit1[rows], scale1[rows], norm1_gain)
        in_grads.append((resid_grad[rows] + pulled).astype(BF16))
        return in_grads[-1]

    gate = query_sum.over_z(gate)
    gate = value_sum.over_x(gate)
    downs[0].over_x_last(gate)
    gate = norm1_pull(0, gate)
    gate = key_sum.over_z(gate)
    gate = norm1_pull(1, gate)
    gate = value_sum.over_z(gate)
    in_grad = jnp.concatenate(in_grads, 0)

    def blocks(vector, lead):
        return jnp.transpose(vector.reshape(lead, dps, -1), (1, 0, 2)).reshape(dps, -1)

    small = jnp.concatenate(
        [
            blocks(norm1_gain_grad, 1),
            blocks(norm1_bias_grad, 1),
            blocks(query_bias_grad, heads_local),
            blocks(value_bias_grad, heads_local),
            blocks(out_bias_grad, 1),
            blocks(norm2_gain_grad, 1),
            blocks(norm2_bias_grad, 1),
            blocks(up_bias_grad, up_bias.shape[0]),
            blocks(down_bias_grad, 1),
        ],
        1,
    )
    small = small.reshape(zs, xs, cs, -1)

    def fold(field, axis, at, dim):
        def take(index):
            return lax.dynamic_index_in_dim(field, index, dim, keepdims=False)

        return take(at) + swap(take(1 - at), axis)

    small = fold(small, "c", at_c, 2)
    small = fold(small, "x", at_x, 1)
    at_z, span = lax.axis_index("z"), zs
    while span > 1:
        span //= 2
        halved = small.reshape(2, span, -1)
        side = (at_z // span) % 2
        pairs = [(i, i ^ span) for i in range(zs)]
        mine = lax.dynamic_index_in_dim(halved, side, 0, keepdims=False)
        other = lax.dynamic_index_in_dim(halved, 1 - side, 0, keepdims=False)
        small = mine + lax.ppermute(other, "z", pairs)
    small = small.reshape(-1)

    down_weight_grad = jnp.concatenate([item.result for item in downs], 0)
    up_weight_grad = jnp.concatenate([item.result for item in ups], 1)

    thin = head_dim // dps
    sizes = [wide, wide, heads_local * thin, heads_local * thin, wide, wide, wide]
    sizes += [up_bias.shape[0] * thin, wide]
    split, begin = [], 0
    for size in sizes:
        split.append(small[begin : begin + size])
        begin += size
    gain1, bias1, query_b, value_b, out_b, gain2, bias2, up_b, down_b = split
    return (
        outputs,
        in_grad,
        gain1,
        bias1,
        query_sum.result,
        query_b.reshape(heads_local, thin),
        key_sum.result,
        value_sum.result,
        value_b.reshape(heads_local, thin),
        out_sum.result,
        out_b,
        gain2,
        bias2,
        up_weight_grad,
        up_b.reshape(-1, thin),
        down_weight_grad,
        down_b,
    )


def solution(mesh):
    dps = mesh.shape["dp"]
    fine = Mesh(mesh.devices.reshape(dps // 4, 2, 2, mesh.shape["mp"]), ("z", "x", "c", "mp"))
    dp = ("z", "x", "c")
    in_specs = (
        P(dp, None),
        P(dp),
        P(),
        P(),
        P(None, "mp"),
        P("mp", None),
        P(None, "mp"),
        P(None, "mp"),
        P("mp", None),
        P("mp", None),
        P(),
        P(),
        P(),
        P(None, "mp"),
        P("mp", None),
        P("mp", None),
        P(),
        P(dp, None),
    )
    out_specs = (
        P(dp, None),
        P(dp, None),
        P(dp),
        P(dp),
        P(dp, "mp"),
        P("mp", dp),
        P(dp, "mp"),
        P(dp, "mp"),
        P("mp", dp),
        P("mp", dp),
        P(dp),
        P(dp),
        P(dp),
        P(dp, "mp"),
        P("mp", dp),
        P("mp", dp),
        P(dp),
    )
    return jax.shard_map(body, mesh=fine, in_specs=in_specs, out_specs=out_specs, check_vma=False)
```
